128 devices in a mesh: mu: 16 (over y, z_hi, core), nu: 8 (over z_lo, x).
Axes of the slice: x: 4, y: 4, z: 4 (z_hi: 2, z_lo: 2; z = z_hi * 2 + z_lo), core: 2. Of those that a mesh axis runs over, the one named last changes fastest.
Arguments:
- earlier_vectors: float32 [1024, 1024, 512], P('mu', 'nu'), may hold values from -0.72 to 0.72
- pivot_integral_columns: float32 [1024, 1024, 256], P('mu', 'nu'), may hold values from -6 to 6
- diagonal: float32 [1024, 1024], P('mu', 'nu'), may hold values from 2 to 60
- orbitals: float32 [1024, 40], replicated, may hold values from -0.1875 to 0.1875
- pivots: int32 [256], replicated, may hold values from 0 to 1048575, as said below
Outputs:
- transformed: float32 [256, 820], P(('mu', 'nu'))
- updated_diagonal: float32 [1024, 1024], P('mu', 'nu')
The draws below stay inside these ranges and needn't reach their ends.
Inputs may be any that keep to these rules, and one draw needn't show every extreme that they name: The pivots are distinct. The pairs held by one device (a block of 64 first by 128 second AO indices) contain at most 8 pivots, and some block contains exactly 8.
All inputs are finite; a program needn't handle non-finite values.
Results may differ from the reference program's by a relative error of at most 0.0001.
Values sent between devices are 32-bit elements; how exact they have to be, the bound alone decides.
No kernel may reach another device: no remote copies, remote signals or barrier semaphores. Data moves between devices by JAX's collectives and lax.ppermute only.
A program may use at most 128 MiB of HBM per device.

```python
import math
import jax
import jax.numpy as jnp
import numpy as np
from jax import lax

NAO = 1024
NVEC = 512
NPIV = 256
NACT = 40
ROWS_MU = 64
COLS_NU = 128
BLOCKS = 128
MOST = 8


def draw_pivots(key, part):
    overall_position_number = BLOCKS * MOST
    hot_count = max(1, NPIV // (4 * MOST))
    key_order, key_score, key_band, key_perm = jax.random.split(jax.random.fold_in(key, 17), 4)
    device_order = jax.random.permutation(key_order, BLOCKS)
    favoured_marker = device_order < hot_count
    position_owner_map = jnp.arange(overall_position_number, dtype=jnp.int32) // MOST
    slot_index = jnp.arange(overall_position_number, dtype=jnp.int32) % MOST
    stochastic_perturbation = jax.random.randint(key_score, (overall_position_number,), 0, 4096)
    preference_increment = jnp.where(favoured_marker[position_owner_map], 8192, 0)
    selection_merit = (stochastic_perturbation + preference_increment) * overall_position_number + jnp.arange(overall_position_number, dtype=jnp.int32)
    top_values, chosen = lax.top_k(selection_merit, NPIV)
    band_size = ROWS_MU * COLS_NU // MOST
    offset = jax.random.randint(key_band, (NPIV,), 0, band_size)
    device = position_owner_map[chosen]
    local_row = slot_index[chosen] * band_size + offset
    grid_nu = NAO // COLS_NU
    row_mu = device // grid_nu * ROWS_MU + local_row // COLS_NU
    col_nu = device % grid_nu * COLS_NU + local_row % COLS_NU
    flat_pair = row_mu * NAO + col_nu
    ordering = jax.random.permutation(key_perm, NPIV)
    return flat_pair[ordering].astype(jnp.int32)


def block_levels(own_key, shape, shards, least, largest):
    def one(position, blocks):
        heights = jax.random.uniform(jax.random.fold_in(jax.random.fold_in(own_key, 6), position), (blocks,), jnp.float32, least / len(shards), largest / len(shards))
        return jnp.repeat(jnp.exp(heights), shape[position] // blocks).reshape((-1,) + (1,) * (len(shape) - position - 1))

    level = one(*shards[0])
    for cut in shards[1:]:
        level = level * one(*cut)
    return level


def normal_values(stream_key, extent, width, most, shards=(), kind=jnp.bfloat16):
    values = jax.random.normal(stream_key, extent, jnp.float32) * width
    if len(shards) > 0:
        values = block_levels(stream_key, extent, shards, -0.22, 0.18) * values
    return jnp.clip(values, min=-most, max=most).astype(kind)


def setup_inputs(seed: int = 0) -> dict:
    arg_keys = jax.random.split(jax.random.key(seed), 6)
    return {
        "earlier_vectors": normal_values(arg_keys[0], (NAO, NAO, NVEC), 0.12, 0.72, ((0, 16), (1, 8)), jnp.float32),
        "pivot_integral_columns": normal_values(arg_keys[1], (NAO, NAO, NPIV), 1.0, 6.0, ((0, 16), (1, 8)), jnp.float32),
        "diagonal": jnp.clip(jnp.exp(math.log(60.0) - 3.4011974 * jax.random.uniform(arg_keys[2], (NAO, NAO), jnp.float32) ** block_levels(arg_keys[2], (NAO, NAO), ((0, 16), (1, 8)), -0.2, 0.2)), 2.0, 60.0),
        "orbitals": normal_values(arg_keys[3], (NAO, NACT), NAO ** -0.5, 0.1875, (), jnp.float32),
        "pivots": draw_pivots(jax.random.fold_in(arg_keys[5], 71), 0),
    }


precise = lax.Precision.HIGHEST

def reference(earlier_vectors, pivot_integral_columns, diagonal, orbitals, pivots):
    row_index, col_index = np.tril_indices(NACT)
    flat_vectors = earlier_vectors.reshape(NAO * NAO, NVEC)
    pivot_rows = jnp.take(flat_vectors, pivots, axis=0)
    pivot_diag = jnp.take(diagonal.reshape(NAO * NAO), pivots)
    residual_diag = pivot_diag - lax.optimization_barrier(jnp.sum(pivot_rows * pivot_rows, axis=1))
    scaling = lax.rsqrt(jnp.maximum(residual_diag, 1.0))
    stride = 32

    def advance(accumulated, start):
        vectors = lax.dynamic_slice_in_dim(earlier_vectors, start, stride, 0).reshape(stride * NAO, NVEC)
        columns = lax.dynamic_slice_in_dim(pivot_integral_columns, start, stride, 0).reshape(stride * NAO, NPIV)
        diag_block = lax.dynamic_slice_in_dim(diagonal, start, stride, 0)
        update = lax.dot_general(vectors, pivot_rows, (((1,), (1,)), ((), ())), precision=precise)
        fresh_vectors = (columns - update) * scaling[None, :]
        new_diag = diag_block - lax.optimization_barrier(jnp.sum(fresh_vectors * fresh_vectors, axis=1)).reshape(stride, NAO)
        orbit_block = lax.dynamic_slice_in_dim(orbitals, start, stride, 0)
        half_done = jnp.einsum('mp,mnj->jpn', orbit_block, fresh_vectors.reshape(stride, NAO, NPIV), precision=precise)
        accumulated = accumulated + jnp.einsum('nq,jpn->jpq', orbitals, half_done, precision=precise)
        return (accumulated, new_diag)
    starts = jnp.arange(NAO // stride, dtype=jnp.int32) * stride
    accumulated, diag_blocks = lax.scan(advance, jnp.zeros((NPIV, NACT, NACT), jnp.float32), starts)
    return (accumulated[:, row_index, col_index], diag_blocks.reshape(NAO, NAO))
```

```python
import jax
import jax.numpy as jnp
import numpy as np
from jax import lax
from jax.sharding import Mesh, PartitionSpec as P

SLOTS = 8
PEERS = ("y", "zh", "zl", "x")
high = lax.Precision.HIGH
exact = lax.Precision.HIGHEST


def exchange(value, axes):
    return lax.all_to_all(value, axes, split_axis=0, concat_axis=0, tiled=True)


def sibling(value):
    return lax.ppermute(value, "c", [(0, 1), (1, 0)])


def owners(pivots):
    chip_mu = pivots >> 17
    core = (pivots >> 16) & 1
    nu = (pivots & 1023) >> 7
    return chip_mu * 8 + nu, core


def local(vectors, columns, diagonal, orbitals, pivots):
    rows, cols, depth = vectors.shape
    count = pivots.shape[0]
    active = orbitals.shape[1]
    chip = lax.axis_index(PEERS)
    core = lax.axis_index("c")
    index_mu = lax.axis_index(("y", "zh", "c"))
    index_nu = lax.axis_index(("zl", "x"))
    own_chip, own_core = owners(pivots)
    block = own_chip * 2 + own_core
    order = jnp.arange(count)
    rank = jnp.sum((block[None, :] == block[:, None]) & (order[None, :] < order[:, None]), axis=1)
    mine = (own_chip == chip) & (own_core == core)
    picks = mine[None, :] & (rank[None, :] == jnp.arange(SLOTS)[:, None])
    local_row = ((pivots >> 10) & 63) * cols + (pivots & 127)
    row = jnp.sum(jnp.where(picks, local_row[None, :], 0), axis=1)
    used = jnp.any(picks, axis=1)
    picked = jnp.where(used[:, None], vectors.reshape(rows * cols, depth)[row], 0.0)
    picked_diag = jnp.where(used, diagonal.reshape(rows * cols)[row], 0.0)
    scale = lax.rsqrt(jnp.maximum(picked_diag - jnp.sum(picked * picked, axis=1), 1.0))
    packed = jnp.concatenate([picked, jnp.broadcast_to(scale[:, None], (SLOTS, 128))], axis=1)
    near = exchange(jnp.broadcast_to(packed[None], (64, SLOTS, depth + 128)), PEERS)
    far = sibling(near)

    left = lax.dynamic_slice_in_dim(orbitals, index_mu * rows, rows, 0)
    right = lax.dynamic_slice_in_dim(orbitals, index_nu * cols, cols, 0)
    row_index, col_index = np.tril_indices(active)

    def transform(value):
        half = jnp.einsum("mp,mnk->pnk", left, value, precision=high)
        full = jnp.einsum("nq,pnk->kpq", right, half, precision=high)
        return full[:, row_index, col_index]

    moved_vectors = transform(vectors)
    moved_columns = transform(columns)
    by_core = moved_columns.reshape(8, 2, 16, -1)
    keep = lax.dynamic_index_in_dim(by_core, core, 1, False).reshape(count // 2, -1)
    give = lax.dynamic_index_in_dim(by_core, 1 - core, 1, False).reshape(count // 2, -1)
    chip_vectors = moved_vectors + sibling(moved_vectors)
    chip_columns = keep + sibling(give)

    place = own_chip * SLOTS + rank
    slot = jnp.arange(64 * SLOTS)
    hot = place[:, None] == slot[None, :]
    near_hot = (hot & (own_core == core)[:, None]).astype(jnp.float32)
    far_hot = (hot & (own_core != core)[:, None]).astype(jnp.float32)
    chosen = jnp.dot(near_hot, near.reshape(64 * SLOTS, -1), precision=exact)
    chosen += jnp.dot(far_hot, far.reshape(64 * SLOTS, -1), precision=exact)
    pivot_rows = chosen[:, :depth]
    scaling = chosen[:, depth]

    home_rows = lax.dynamic_index_in_dim(chosen.reshape(8, 2, 16, -1), core, 1, False).reshape(count // 2, -1)
    part = chip_columns - jnp.dot(home_rows[:, :depth], chip_vectors, precision=high)
    part = part * home_rows[:, depth : depth + 1]
    arrived = exchange(part.reshape(64, 2, -1), PEERS)
    transformed = arrived.sum(axis=0)

    update = jnp.einsum("mnk,jk->mnj", vectors, pivot_rows, precision=high)
    fresh = (columns - update) * scaling
    updated = diagonal - jnp.sum(fresh * fresh, axis=2)
    return transformed, updated


def solution(mesh):
    fine = Mesh(mesh.devices.reshape(4, 2, 2, 2, 4), ("y", "zh", "c", "zl", "x"))
    mu, nu = ("y", "zh", "c"), ("zl", "x")
    placed = (P(mu, nu, None), P(mu, nu, None), P(mu, nu), P(), P())
    return jax.shard_map(
        local,
        mesh=fine,
        in_specs=placed,
        out_specs=(P(mu + nu, None), P(mu, nu)),
        check_vma=False,
    )
```

```python
import functools

import jax
import jax.numpy as jnp
from jax import lax
from jax.experimental import pallas as pl
from jax.experimental.pallas import tpu as pltpu
from jax.sharding import Mesh, PartitionSpec as P

SLOTS = 8
LANES = 128
PEERS = ("y", "zh", "zl", "x")
f32, bf16 = jnp.float32, jnp.bfloat16
smem = pl.BlockSpec(memory_space=pltpu.SMEM)
vmem = pl.BlockSpec(memory_space=pltpu.VMEM)
hbm = pl.BlockSpec(memory_space=pl.ANY)


def exchange(value, axes):
    return lax.all_to_all(value, axes, split_axis=0, concat_axis=0, tiled=True)


def sibling(value):
    return lax.ppermute(value, "c", [(0, 1), (1, 0)])


def iota(shape, dim):
    return lax.broadcasted_iota(jnp.int32, shape, dim)


def split(value):
    upper = value.astype(bf16)
    return upper, (value - upper.astype(f32)).astype(bf16)


def dot(a, b):
    return jnp.dot(a, b, preferred_element_type=f32)


def dot_nt(a, b):
    return lax.dot_general(a, b, (((1,), (1,)), ((), ())), preferred_element_type=f32)


def params(mib):
    return pltpu.CompilerParams(vmem_limit_bytes=mib << 20)


def pick_kernel(me, pivots, diagonal, vectors, out, rows, spots, index, sems):
    count = pivots.shape[0]
    cols, depth = vectors.shape[1:]
    for slot in range(2 * SLOTS):
        index[slot] = 0

    def scan(j, found):
        pair = pivots[j]
        index[found] = ((pair >> 10) & 63) * cols + (pair & 127)
        owner = (pair >> 16) * 8 + ((pair & 1023) >> 7)
        return found + (owner == me[0]).astype(jnp.int32)

    found = lax.fori_loop(0, count, scan, 0, unroll=8)
    copies = []
    for slot in range(SLOTS):
        spot = index[slot]
        copies.append(
            pltpu.make_async_copy(
                vectors.at[spot >> 7, pl.ds(spot & 127, 1), :],
                rows.at[pl.ds(slot, 1), :],
                sems.at[slot],
            )
        )
        copies[-1].start()
    lane = iota((1, LANES), 1)
    for slot in range(SLOTS):
        spot = index[slot]
        line = diagonal[pl.ds(spot >> 7, 1), :]
        spots[pl.ds(slot, 1), :] = jnp.where(lane == (spot & 127), line, 0.0)
    for copy in copies:
        copy.wait()
    used = iota((SLOTS, 1), 0) < found
    picked = jnp.where(used, rows[...], 0.0)
    residual = jnp.sum(spots[...], axis=1, keepdims=True) - jnp.sum(picked * picked, axis=1, keepdims=True)
    scale = lax.rsqrt(jnp.maximum(jnp.where(used, residual, 1.0), 1.0))
    out[:, :, :depth] = jnp.broadcast_to(picked[None], (64, SLOTS, depth))
    out[:, :, depth:] = jnp.broadcast_to(scale[None], (64, SLOTS, LANES))


def pick(me, pivots, diagonal, vectors):
    depth = vectors.shape[2]
    return pl.pallas_call(
        pick_kernel,
        out_shape=jax.ShapeDtypeStruct((64, SLOTS, depth + LANES), f32),
        in_specs=[smem, smem, vmem, hbm],
        out_specs=vmem,
        scratch_shapes=[
            pltpu.VMEM((SLOTS, depth), f32),
            pltpu.VMEM((SLOTS, LANES), f32),
            pltpu.SMEM((2 * SLOTS,), jnp.int32),
            pltpu.SemaphoreType.DMA((SLOTS,)),
        ],
        name="pick",
    )(me, pivots, diagonal, vectors)


def transform_kernel(flip, me, orbitals, value, out, wide_hi, wide_lo, right2, half, square, *flat):
    step = pl.program_id(0)
    tall, cols, width = value.shape
    rows = half.shape[0]
    active = orbitals.shape[1]

    @pl.when(step == 0)
    def _():
        left = orbitals[pl.ds(pl.multiple_of((me[0] >> 3) * rows, rows), rows), :]
        right = orbitals[pl.ds(pl.multiple_of((me[0] & 7) * cols, cols), cols), :]
        high = (active * 8, active)
        spread_rows = jnp.where(iota(high, 0) // 8 == iota(high, 1), 1.0, 0.0).astype(bf16)
        long = (rows, rows * 8)
        spread_cols = jnp.where(iota(long, 0) == iota(long, 1) // 8, 1.0, 0.0).astype(bf16)
        full = (active * 8, rows * 8)
        same = iota(full, 0) % 8 == iota(full, 1) % 8
        for part, wide in zip(split(left), (wide_hi, wide_lo)):
            repeated = dot(dot_nt(spread_rows, part).astype(bf16), spread_cols)
            wide[...] = jnp.where(same, repeated, 0.0).astype(bf16)
        eye = jnp.where(iota((48, active), 0) == iota((48, active), 1), 1.0, 0.0).astype(bf16)
        upper, lower = [dot_nt(eye, part).astype(bf16) for part in split(right)]
        right2[:48, :cols] = upper
        right2[:48, cols:] = upper
        right2[48:, :cols] = lower
        right2[48:, cols:] = jnp.zeros_like(lower)

    for i in range(tall):
        both = dot(right2[...], jnp.concatenate(split(value[i]), axis=0))
        half[step * tall + i] = both[:active] + both[48 : 48 + active]

    target = flat[0] if flip else out

    @pl.when(step == pl.num_programs(0) - 1)
    def _():
        for q in range(0, active, 8):
            upper, lower = split(half[:, q : q + 8, :].reshape(rows * 8, width))
            hi, lo = wide_hi[8 * q :, :], wide_lo[8 * q :, :]
            part = dot(hi, upper) + dot(lo, upper) + dot(hi, lower)
            square[q:, q : q + 8, :] = part.reshape(active - q, 8, width)
        for p in range(active):
            target[p * (p + 1) // 2 : (p + 1) * (p + 2) // 2, :] = square[p, : p + 1, :]
        if flip:
            turned = target[...].T[:, : out.shape[2]]
            for i in range(8):
                for c in range(2):
                    out[c, 16 * i : 16 * i + 16, :] = turned[32 * i + 16 * c : 32 * i + 16 * c + 16, :]


def transform(me, orbitals, value, flip):
    rows, cols, width = value.shape
    active = orbitals.shape[1]
    pairs = active * (active + 1) // 2
    tall = 8
    shape = (2, width // 2, pairs) if flip else (pairs, width)
    scratch = [
        pltpu.VMEM((active * 8, rows * 8), bf16),
        pltpu.VMEM((active * 8, rows * 8), bf16),
        pltpu.VMEM((96, 2 * cols), bf16),
        pltpu.VMEM((rows, active, width), f32),
        pltpu.VMEM((active, active, width), f32),
    ]
    if flip:
        scratch.append(pltpu.VMEM((pl.cdiv(pairs, LANES) * LANES, width), f32))
    return pl.pallas_call(
        functools.partial(transform_kernel, flip),
        out_shape=jax.ShapeDtypeStruct(shape, f32),
        grid=(rows // tall,),
        in_specs=[
            smem,
            pl.BlockSpec(orbitals.shape, lambda i: (0, 0)),
            pl.BlockSpec((tall, cols, width), lambda i: (i, 0, 0)),
        ],
        out_specs=pl.BlockSpec(shape, lambda i: (0,) * len(shape)),
        scratch_shapes=scratch,
        compiler_params=params(52),
        cost_estimate=pl.CostEstimate(
            flops=6 * active * 8 * rows * 8 * width * 16, bytes_accessed=value.size * 4, transcendentals=0
        ),
        name="turn_columns" if flip else "turn_vectors",
    )(me, orbitals, value)


def choose_kernel(me, near_hot, far_hot, near, far, upper_v, lower_v, mine_c, got_c, part, rows_hi, rows_lo, scaling, keep_hi, keep_lo):
    slots, width = near.shape
    depth = width - LANES
    core = (me[0] >> 3) & 1
    near_hi, near_lo = split(near[...])
    far_hi, far_lo = split(far[...])
    hi = dot(near_hot[...], near_hi) + dot(far_hot[...], far_hi)
    lo = dot(near_hot[...], near_lo) + dot(far_hot[...], far_lo)
    hi16, lo16 = hi.astype(bf16), lo.astype(bf16)
    rows_hi[...] = hi16[:, :depth]
    rows_lo[...] = lo16[:, :depth]
    scale = hi[:, depth:] + lo[:, depth:]
    scaling[...] = scale.T[:8]
    keep_hi[...] = hi16.reshape(keep_hi.shape)
    keep_lo[...] = lo16.reshape(keep_lo.shape)
    home_hi = keep_hi[:, core].reshape(-1, width)
    home_lo = keep_lo[:, core].reshape(-1, width)
    moved = (
        dot_nt(home_hi[:, :depth], upper_v[...])
        + dot_nt(home_lo[:, :depth], upper_v[...])
        + dot_nt(home_hi[:, :depth], lower_v[...])
    )
    scale = home_hi[:, depth : depth + 1].astype(f32) + home_lo[:, depth : depth + 1].astype(f32)
    part[...] = (mine_c[core] + got_c[...] - moved) * scale


def choose(me, near_hot, far_hot, near, far, upper_v, lower_v, mine_c, got_c):
    count, slots = near_hot.shape
    width = near.shape[1]
    depth = width - LANES
    pairs = upper_v.shape[0]
    return pl.pallas_call(
        choose_kernel,
        out_shape=(
            jax.ShapeDtypeStruct((count // 2, pairs), f32),
            jax.ShapeDtypeStruct((count, depth), bf16),
            jax.ShapeDtypeStruct((count, depth), bf16),
            jax.ShapeDtypeStruct((8, count), f32),
        ),
        in_specs=[smem] + [vmem] * 8,
        out_specs=(vmem,) * 4,
        scratch_shapes=[pltpu.VMEM((8, 2, 16, width), bf16), pltpu.VMEM((8, 2, 16, width), bf16)],
        compiler_params=params(24),
        cost_estimate=pl.CostEstimate(flops=2 * 10**9, bytes_accessed=6 * 10**6, transcendentals=0),
        name="choose",
    )(me, near_hot, far_hot, near, far, upper_v, lower_v, mine_c, got_c)


def update_kernel(vectors, columns, diagonal, rows_hi, rows_lo, scaling, out):
    tall, cols, depth = vectors.shape
    count = columns.shape[2]
    upper, lower = split(vectors[...].reshape(tall * cols, depth))
    update = dot_nt(upper, rows_hi[...]) + dot_nt(lower, rows_hi[...]) + dot_nt(upper, rows_lo[...])
    fresh = (columns[...].reshape(tall * cols, count) - update) * scaling[:1, :]
    square = fresh * fresh
    folded = (square[:, :LANES] + square[:, LANES:]).reshape(tall, cols, LANES)
    out[...] = diagonal[...] - jnp.sum(jnp.swapaxes(folded, 1, 2), axis=1)


def update(vectors, columns, diagonal, rows_hi, rows_lo, scaling):
    rows, cols, depth = vectors.shape
    count = columns.shape[2]
    tall = 8
    return pl.pallas_call(
        update_kernel,
        out_shape=jax.ShapeDtypeStruct((rows, cols), f32),
        grid=(rows // tall,),
        in_specs=[
            pl.BlockSpec((tall, cols, depth), lambda i: (i, 0, 0)),
            pl.BlockSpec((tall, cols, count), lambda i: (i, 0, 0)),
            pl.BlockSpec((tall, cols), lambda i: (i, 0)),
            pl.BlockSpec((count, depth), lambda i: (0, 0)),
            pl.BlockSpec((count, depth), lambda i: (0, 0)),
            pl.BlockSpec((8, count), lambda i: (0, 0)),
        ],
        out_specs=pl.BlockSpec((tall, cols), lambda i: (i, 0)),
        compiler_params=params(52),
        cost_estimate=pl.CostEstimate(
            flops=6 * rows * cols * depth * count, bytes_accessed=4 * (vectors.size + columns.size), transcendentals=0
        ),
        name="update",
    )(vectors, columns, diagonal, rows_hi, rows_lo, scaling)


def local(vectors, columns, diagonal, orbitals, pivots):
    depth = vectors.shape[2]
    count = pivots.shape[0]
    core = lax.axis_index("c")
    me = lax.axis_index(("y", "zh", "c", "zl", "x")).reshape(1)
    near = exchange(pick(me, pivots, diagonal, vectors), PEERS)

    own_chip, own_core = (pivots >> 17) * 8 + ((pivots & 1023) >> 7), (pivots >> 16) & 1
    block = own_chip * 2 + own_core
    order = jnp.arange(count)
    rank = jnp.sum((block[None, :] == block[:, None]) & (order[None, :] < order[:, None]), axis=1)
    place = jnp.where(own_core == core, own_chip * SLOTS + rank, -1)
    other = jnp.where(own_core == core, -1, own_chip * SLOTS + rank)
    slot = jnp.arange(64 * SLOTS)
    near_hot = (place[:, None] == slot[None, :]).astype(bf16)
    far_hot = (other[:, None] == slot[None, :]).astype(bf16)

    mine_v = transform(me, orbitals, vectors, False)
    got_v = sibling(mine_v)
    mine_c = transform(me, orbitals, columns, True)
    got_c = sibling(lax.dynamic_index_in_dim(mine_c, 1 - core, 0, False))
    chip_v = mine_v + got_v
    upper_v = lax.reduce_precision(chip_v, 8, 7)
    lower_v = (chip_v - upper_v).astype(bf16)
    upper_v = upper_v.astype(bf16)

    far = sibling(near)
    flat = (64 * SLOTS, depth + LANES)
    part, rows_hi, rows_lo, scaling = choose(
        me, near_hot, far_hot, near.reshape(flat), far.reshape(flat), upper_v, lower_v, mine_c, got_c
    )
    arrived = exchange(part, PEERS).reshape(64, 2, -1)
    updated = update(vectors, columns, diagonal, rows_hi, rows_lo, scaling)
    return arrived.sum(axis=0), updated


def solution(mesh):
    fine = Mesh(mesh.devices.reshape(4, 2, 2, 2, 4), ("y", "zh", "c", "zl", "x"))
    mu, nu = ("y", "zh", "c"), ("zl", "x")
    placed = (P(mu, nu, None), P(mu, nu, None), P(mu, nu), P(), P())
    return jax.shard_map(
        local,
        mesh=fine,
        in_specs=placed,
        out_specs=(P(mu + nu, None), P(mu, nu)),
        check_vma=False,
    )
```

```python
import functools

import jax
import jax.numpy as jnp
from jax import lax
from jax.experimental import pallas as pl
from jax.experimental.pallas import tpu as pltpu
from jax.sharding import Mesh, PartitionSpec as P

SLOTS = 8
LANES = 128
PEERS = ("y", "zh", "zl", "x")
f32, bf16 = jnp.float32, jnp.bfloat16
smem = pl.BlockSpec(memory_space=pltpu.SMEM)
vmem = pl.BlockSpec(memory_space=pltpu.VMEM)
hbm = pl.BlockSpec(memory_space=pl.ANY)


def exchange(value, axes):
    return lax.all_to_all(value, axes, split_axis=0, concat_axis=0, tiled=True)


def sibling(value):
    return lax.ppermute(value, "c", [(0, 1), (1, 0)])


def iota(shape, dim):
    return lax.broadcasted_iota(jnp.int32, shape, dim)


def split(value):
    upper = value.astype(bf16)
    return upper, (value - upper.astype(f32)).astype(bf16)


def dot(a, b):
    return jnp.dot(a, b, preferred_element_type=f32)


def dot_nt(a, b):
    return lax.dot_general(a, b, (((1,), (1,)), ((), ())), preferred_element_type=f32)


def params(mib):
    return pltpu.CompilerParams(vmem_limit_bytes=mib << 20)


def pick_kernel(me, pivots, diagonal, vectors, out, rows, spots, index, sems):
    count = pivots.shape[0]
    cols, depth = vectors.shape[1:]
    for slot in range(2 * SLOTS):
        index[slot] = 0
    key = (me[0] >> 3) * 65536 + (me[0] & 7) * LANES
    group = 16

    def scan(i, found):
        pairs = [pivots[i * group + j] for j in range(group)]
        owned = [((pair & 0xF0380) == key).astype(jnp.int32) for pair in pairs]
        for pair, own in zip(pairs, owned):
            index[found] = ((pair >> 10) & 63) * cols + (pair & 127)
            found = found + own
        return found

    found = lax.fori_loop(0, count // group, scan, 0)
    copies = []
    for slot in range(SLOTS):
        spot = index[slot]
        copies.append(
            pltpu.make_async_copy(
                vectors.at[spot >> 7, pl.ds(spot & 127, 1), :],
                rows.at[pl.ds(slot, 1), :],
                sems.at[slot],
            )
        )
        copies[-1].start()
    lane = iota((1, LANES), 1)
    for slot in range(SLOTS):
        spot = index[slot]
        line = diagonal[pl.ds(spot >> 7, 1), :]
        spots[pl.ds(slot, 1), :] = jnp.where(lane == (spot & 127), line, 0.0)
    for copy in copies:
        copy.wait()
    used = iota((SLOTS, 1), 0) < found
    picked = jnp.where(used, rows[...], 0.0)
    residual = jnp.sum(spots[...], axis=1, keepdims=True) - jnp.sum(picked * picked, axis=1, keepdims=True)
    scale = lax.rsqrt(jnp.maximum(jnp.where(used, residual, 1.0), 1.0))
    out[:, :, :depth] = jnp.broadcast_to(picked[None], (64, SLOTS, depth))
    out[:, :, depth:] = jnp.broadcast_to(scale[None], (64, SLOTS, LANES))


def pick(me, pivots, diagonal, vectors):
    depth = vectors.shape[2]
    return pl.pallas_call(
        pick_kernel,
        out_shape=jax.ShapeDtypeStruct((64, SLOTS, depth + LANES), f32),
        in_specs=[smem, smem, vmem, hbm],
        out_specs=vmem,
        scratch_shapes=[
            pltpu.VMEM((SLOTS, depth), f32),
            pltpu.VMEM((SLOTS, LANES), f32),
            pltpu.SMEM((2 * SLOTS,), jnp.int32),
            pltpu.SemaphoreType.DMA((SLOTS,)),
        ],
        name="pick",
    )(me, pivots, diagonal, vectors)


def transform_kernel(flip, me, turned_orbitals, value, out, block, wide_hi, wide_lo, right2, half, square, sems, *flat):
    rows, cols, width = block.shape
    active = turned_orbitals.shape[0]
    steps = sems.shape[0]
    tall = rows // steps

    def fetch(step):
        part = pl.ds(step * tall, tall)
        return pltpu.make_async_copy(value.at[part], block.at[part], sems.at[step])

    for step in range(steps):
        fetch(step).start()

    index_mu = me[0] >> 3
    left = turned_orbitals[:, pl.ds(pl.multiple_of((index_mu >> 1) * LANES, LANES), LANES)]
    right = turned_orbitals[:, pl.ds(pl.multiple_of((me[0] & 7) * cols, cols), cols)]
    high = (active * 8, active)
    spread_rows = jnp.where(iota(high, 0) // 8 == iota(high, 1), 1.0, 0.0).astype(bf16)
    long = (LANES, rows * 8)
    spread_cols = jnp.where(iota(long, 0) == iota(long, 1) // 8 + (index_mu & 1) * rows, 1.0, 0.0).astype(bf16)
    full = (active * 8, rows * 8)
    same = iota(full, 0) % 8 == iota(full, 1) % 8
    for part, wide in zip(split(left), (wide_hi, wide_lo)):
        repeated = dot(dot(spread_rows, part).astype(bf16), spread_cols)
        wide[...] = jnp.where(same, repeated, 0.0).astype(bf16)
    eye = jnp.where(iota((48, active), 0) == iota((48, active), 1), 1.0, 0.0).astype(bf16)
    upper, lower = [dot(eye, part).astype(bf16) for part in split(right)]
    right2[:48, :cols] = upper
    right2[:48, cols:] = upper
    right2[48:, :cols] = lower
    right2[48:, cols:] = jnp.zeros_like(lower)

    def advance(step, carry):
        fetch(step).wait()
        for i in range(tall):
            row = step * tall + i
            both = dot(right2[...], jnp.concatenate(split(block[row]), axis=0))
            half[row] = both[:active] + both[48 : 48 + active]
        return carry

    lax.fori_loop(0, steps, advance, 0)
    target = flat[0] if flip else out
    for q in range(0, active, 8):
        upper, lower = split(half[:, q : q + 8, :].reshape(rows * 8, width))
        hi, lo = wide_hi[8 * q :, :], wide_lo[8 * q :, :]
        both = dot(jnp.concatenate([hi, lo], axis=0), upper)
        part = both[: 8 * (active - q)] + both[8 * (active - q) :] + dot(hi, lower)
        square[q:, q : q + 8, :] = part.reshape(active - q, 8, width)
    for p in range(active):
        target[p * (p + 1) // 2 : (p + 1) * (p + 2) // 2, :] = square[p, : p + 1, :]
    if flip:
        turned = target[...].T[:, : out.shape[2]]
        for i in range(8):
            for c in range(2):
                out[c, 16 * i : 16 * i + 16, :] = turned[32 * i + 16 * c : 32 * i + 16 * c + 16, :]


def transform(me, turned_orbitals, value, flip):
    rows, cols, width = value.shape
    active = turned_orbitals.shape[0]
    pairs = active * (active + 1) // 2
    steps = 8
    shape = (2, width // 2, pairs) if flip else (pairs, width)
    scratch = [
        pltpu.VMEM(value.shape, f32),
        pltpu.VMEM((active * 8, rows * 8), bf16),
        pltpu.VMEM((active * 8, rows * 8), bf16),
        pltpu.VMEM((96, 2 * cols), bf16),
        pltpu.VMEM((rows, active, width), f32),
        pltpu.VMEM((active, active, width), f32),
        pltpu.SemaphoreType.DMA((steps,)),
    ]
    if flip:
        scratch.append(pltpu.VMEM((pl.cdiv(pairs, LANES) * LANES, width), f32))
    return pl.pallas_call(
        functools.partial(transform_kernel, flip),
        out_shape=jax.ShapeDtypeStruct(shape, f32),
        in_specs=[smem, vmem, hbm],
        out_specs=vmem,
        scratch_shapes=scratch,
        compiler_params=params(56),
        cost_estimate=pl.CostEstimate(
            flops=6 * active * 8 * rows * 8 * width * 16, bytes_accessed=value.size * 4, transcendentals=0
        ),
        name="turn_columns" if flip else "turn_vectors",
    )(me, turned_orbitals, value)


def choose_kernel(me, near_hot, far_hot, near, far, upper_v, lower_v, mine_c, got_c, part, rows_hi, rows_lo, scaling, keep_hi, keep_lo):
    slots, width = near.shape
    depth = width - LANES
    core = (me[0] >> 3) & 1
    near_hi, near_lo = split(near[...])
    far_hi, far_lo = split(far[...])
    hi = dot(near_hot[...], near_hi) + dot(far_hot[...], far_hi)
    lo = dot(near_hot[...], near_lo) + dot(far_hot[...], far_lo)
    hi16, lo16 = hi.astype(bf16), lo.astype(bf16)
    rows_hi[...] = hi16[:, :depth]
    rows_lo[...] = lo16[:, :depth]
    scale = hi[:, depth:] + lo[:, depth:]
    scaling[...] = scale.T[:8]
    keep_hi[...] = hi16.reshape(keep_hi.shape)
    keep_lo[...] = lo16.reshape(keep_lo.shape)
    home_hi = keep_hi[:, core].reshape(-1, width)
    home_lo = keep_lo[:, core].reshape(-1, width)
    moved = (
        dot_nt(home_hi[:, :depth], upper_v[...])
        + dot_nt(home_lo[:, :depth], upper_v[...])
        + dot_nt(home_hi[:, :depth], lower_v[...])
    )
    scale = home_hi[:, depth : depth + 1].astype(f32) + home_lo[:, depth : depth + 1].astype(f32)
    part[...] = (mine_c[core] + got_c[...] - moved) * scale


def choose(me, near_hot, far_hot, near, far, upper_v, lower_v, mine_c, got_c):
    count, slots = near_hot.shape
    width = near.shape[1]
    depth = width - LANES
    pairs = upper_v.shape[0]
    return pl.pallas_call(
        choose_kernel,
        out_shape=(
            jax.ShapeDtypeStruct((count // 2, pairs), f32),
            jax.ShapeDtypeStruct((count, depth), bf16),
            jax.ShapeDtypeStruct((count, depth), bf16),
            jax.ShapeDtypeStruct((8, count), f32),
        ),
        in_specs=[smem] + [vmem] * 8,
        out_specs=(vmem,) * 4,
        scratch_shapes=[pltpu.VMEM((8, 2, 16, width), bf16), pltpu.VMEM((8, 2, 16, width), bf16)],
        compiler_params=params(24),
        cost_estimate=pl.CostEstimate(flops=2 * 10**9, bytes_accessed=6 * 10**6, transcendentals=0),
        name="choose",
    )(me, near_hot, far_hot, near, far, upper_v, lower_v, mine_c, got_c)


def update_kernel(vectors, columns, diagonal, rows_hi, rows_lo, scaling, out, block, beside, sems):
    rows, cols, depth = block.shape
    count = beside.shape[2]
    steps = sems.shape[1]
    tall = rows // steps

    def fetch(step):
        part = pl.ds(step * tall, tall)
        return (
            pltpu.make_async_copy(vectors.at[part], block.at[part], sems.at[0, step]),
            pltpu.make_async_copy(columns.at[part], beside.at[part], sems.at[1, step]),
        )

    for step in range(steps):
        for copy in fetch(step):
            copy.start()

    def advance(step, carry):
        for copy in fetch(step):
            copy.wait()
        part = pl.ds(pl.multiple_of(step * tall, tall), tall)
        upper, lower = split(block[part].reshape(tall * cols, depth))
        update = dot_nt(upper, rows_hi[...]) + dot_nt(lower, rows_hi[...]) + dot_nt(upper, rows_lo[...])
        fresh = (beside[part].reshape(tall * cols, count) - update) * scaling[:1, :]
        square = fresh * fresh
        folded = (square[:, :LANES] + square[:, LANES:]).reshape(tall, cols, LANES)
        out[part, :] = diagonal[part, :] - jnp.sum(jnp.swapaxes(folded, 1, 2), axis=1)
        return carry

    lax.fori_loop(0, steps, advance, 0)


def update(vectors, columns, diagonal, rows_hi, rows_lo, scaling):
    rows, cols, depth = vectors.shape
    count = columns.shape[2]
    steps = 8
    return pl.pallas_call(
        update_kernel,
        out_shape=jax.ShapeDtypeStruct((rows, cols), f32),
        in_specs=[hbm, hbm, vmem, vmem, vmem, vmem],
        out_specs=vmem,
        scratch_shapes=[
            pltpu.VMEM(vectors.shape, f32),
            pltpu.VMEM(columns.shape, f32),
            pltpu.SemaphoreType.DMA((2, steps)),
        ],
        compiler_params=params(56),
        cost_estimate=pl.CostEstimate(
            flops=6 * rows * cols * depth * count, bytes_accessed=4 * (vectors.size + columns.size), transcendentals=0
        ),
        name="update",
    )(vectors, columns, diagonal, rows_hi, rows_lo, scaling)


def local(vectors, columns, diagonal, orbitals, pivots):
    depth = vectors.shape[2]
    count = pivots.shape[0]
    core = lax.axis_index("c")
    me = lax.axis_index(("y", "zh", "c", "zl", "x")).reshape(1)
    near = exchange(pick(me, pivots, diagonal, vectors), PEERS)

    own_chip, own_core = (pivots >> 17) * 8 + ((pivots & 1023) >> 7), (pivots >> 16) & 1
    block = own_chip * 2 + own_core
    order = jnp.arange(count)
    rank = jnp.sum((block[None, :] == block[:, None]) & (order[None, :] < order[:, None]), axis=1)
    place = jnp.where(own_core == core, own_chip * SLOTS + rank, -1)
    other = jnp.where(own_core == core, -1, own_chip * SLOTS + rank)
    slot = jnp.arange(64 * SLOTS)
    near_hot = (place[:, None] == slot[None, :]).astype(bf16)
    far_hot = (other[:, None] == slot[None, :]).astype(bf16)

    orbitals = orbitals.T
    mine_v = transform(me, orbitals, vectors, False)
    got_v = sibling(mine_v)
    mine_c = transform(me, orbitals, columns, True)
    near, mine_c = lax.optimization_barrier((near, mine_c))
    got_c = sibling(lax.dynamic_index_in_dim(mine_c, 1 - core, 0, False))
    chip_v = mine_v + got_v
    upper_v = lax.reduce_precision(chip_v, 8, 7)
    lower_v = (chip_v - upper_v).astype(bf16)
    upper_v = upper_v.astype(bf16)

    far = sibling(near)
    flat = (64 * SLOTS, depth + LANES)
    part, rows_hi, rows_lo, scaling = choose(
        me, near_hot, far_hot, near.reshape(flat), far.reshape(flat), upper_v, lower_v, mine_c, got_c
    )
    arrived = exchange(part, PEERS).reshape(64, 2, -1)
    updated = update(vectors, columns, diagonal, rows_hi, rows_lo, scaling)
    return arrived.sum(axis=0), updated


def solution(mesh):
    fine = Mesh(mesh.devices.reshape(4, 2, 2, 2, 4), ("y", "zh", "c", "zl", "x"))
    mu, nu = ("y", "zh", "c"), ("zl", "x")
    placed = (P(mu, nu, None), P(mu, nu, None), P(mu, nu), P(), P())
    return jax.shard_map(
        local,
        mesh=fine,
        in_specs=placed,
        out_specs=(P(mu + nu, None), P(mu, nu)),
        check_vma=False,
    )
```

```python
import functools

import jax
import jax.numpy as jnp
from jax import lax
from jax.experimental import pallas as pl
from jax.experimental.pallas import tpu as pltpu
from jax.sharding import Mesh, PartitionSpec as P

SLOTS = 8
LANES = 128
PEERS = ("y", "zh", "zl", "x")
f32, bf16 = jnp.float32, jnp.bfloat16
smem = pl.BlockSpec(memory_space=pltpu.SMEM)
vmem = pl.BlockSpec(memory_space=pltpu.VMEM)
hbm = pl.BlockSpec(memory_space=pl.ANY)


def exchange(value, axes):
    return lax.all_to_all(value, axes, split_axis=0, concat_axis=0, tiled=True)


def sibling(value):
    return lax.ppermute(value, "c", [(0, 1), (1, 0)])


def iota(shape, dim):
    return lax.broadcasted_iota(jnp.int32, shape, dim)


def split(value):
    upper = value.astype(bf16)
    return upper, (value - upper.astype(f32)).astype(bf16)


def dot(a, b):
    return jnp.dot(a, b, preferred_element_type=f32)


def dot_nt(a, b):
    return lax.dot_general(a, b, (((1,), (1,)), ((), ())), preferred_element_type=f32)


def params(mib):
    return pltpu.CompilerParams(vmem_limit_bytes=mib << 20)


def pick_kernel(me, pivots, diagonal, vectors, out, rows, spots, index, sems):
    count = pivots.shape[0]
    cols, depth = vectors.shape[1:]
    for slot in range(2 * SLOTS):
        index[slot] = 0
    key = (me[0] >> 3) * 65536 + (me[0] & 7) * LANES
    group = 16

    def scan(i, found):
        pairs = [pivots[i * group + j] for j in range(group)]
        owned = [((pair & 0xF0380) == key).astype(jnp.int32) for pair in pairs]
        for pair, own in zip(pairs, owned):
            index[found] = ((pair >> 10) & 63) * cols + (pair & 127)
            found = found + own
        return found

    found = lax.fori_loop(0, count // group, scan, 0)
    copies = []
    for slot in range(SLOTS):
        spot = index[slot]
        copies.append(
            pltpu.make_async_copy(
                vectors.at[spot >> 7, pl.ds(spot & 127, 1), :],
                rows.at[pl.ds(slot, 1), :],
                sems.at[slot],
            )
        )
        copies[-1].start()
    lane = iota((1, LANES), 1)
    for slot in range(SLOTS):
        spot = index[slot]
        line = diagonal[pl.ds(spot >> 7, 1), :]
        spots[pl.ds(slot, 1), :] = jnp.where(lane == (spot & 127), line, 0.0)
    for copy in copies:
        copy.wait()
    used = iota((SLOTS, 1), 0) < found
    picked = jnp.where(used, rows[...], 0.0)
    residual = jnp.sum(spots[...], axis=1, keepdims=True) - jnp.sum(picked * picked, axis=1, keepdims=True)
    scale = lax.rsqrt(jnp.maximum(jnp.where(used, residual, 1.0), 1.0))
    out[:, :, :depth] = jnp.broadcast_to(picked[None], (64, SLOTS, depth))
    out[:, :, depth:] = jnp.broadcast_to(scale[None], (64, SLOTS, LANES))


def pick(me, pivots, diagonal, vectors):
    depth = vectors.shape[2]
    return pl.pallas_call(
        pick_kernel,
        out_shape=jax.ShapeDtypeStruct((64, SLOTS, depth + LANES), f32),
        in_specs=[smem, smem, vmem, hbm],
        out_specs=vmem,
        scratch_shapes=[
            pltpu.VMEM((SLOTS, depth), f32),
            pltpu.VMEM((SLOTS, LANES), f32),
            pltpu.SMEM((2 * SLOTS,), jnp.int32),
            pltpu.SemaphoreType.DMA((SLOTS,)),
        ],
        name="pick",
    )(me, pivots, diagonal, vectors)


def turn_kernel(
    me, turned_orbitals, vectors, columns, out, keep, give, block, beside, wide_hi, wide_lo, right2, half, square, flat, sems
):
    rows, cols, _ = block.shape
    active, pairs = turned_orbitals.shape[0], out.shape[0]
    steps = sems.shape[1]
    tall = rows // steps

    def fetch(kind, step):
        part = pl.ds(step * tall, tall)
        source, target = ((vectors, block), (columns, beside))[kind]
        return pltpu.make_async_copy(source.at[part], target.at[part], sems.at[kind, step])

    for kind in range(2):
        for step in range(steps):
            fetch(kind, step).start()

    index_mu = me[0] >> 3
    left = turned_orbitals[:, pl.ds(pl.multiple_of((index_mu >> 1) * LANES, LANES), LANES)]
    right = turned_orbitals[:, pl.ds(pl.multiple_of((me[0] & 7) * cols, cols), cols)]
    high = (active * 8, active)
    spread_rows = jnp.where(iota(high, 0) // 8 == iota(high, 1), 1.0, 0.0).astype(bf16)
    long = (LANES, rows * 8)
    spread_cols = jnp.where(iota(long, 0) == iota(long, 1) // 8 + (index_mu & 1) * rows, 1.0, 0.0).astype(bf16)
    full = (active * 8, rows * 8)
    same = iota(full, 0) % 8 == iota(full, 1) % 8
    for part, wide in zip(split(left), (wide_hi, wide_lo)):
        repeated = dot(dot(spread_rows, part).astype(bf16), spread_cols)
        wide[...] = jnp.where(same, repeated, 0.0).astype(bf16)
    eye = jnp.where(iota((48, active), 0) == iota((48, active), 1), 1.0, 0.0).astype(bf16)
    upper, lower = [dot(eye, part).astype(bf16) for part in split(right)]
    right2[:48, :cols] = upper
    right2[:48, cols:] = upper
    right2[48:, :cols] = lower
    right2[48:, cols:] = jnp.zeros_like(lower)

    for kind, (value, target) in enumerate(((block, out), (beside, flat))):
        width = value.shape[2]

        def advance(step, carry):
            fetch(kind, step).wait()
            for i in range(tall):
                row = step * tall + i
                both = dot(right2[...], jnp.concatenate(split(value[row]), axis=0))
                half[row, :, :width] = both[:active] + both[48 : 48 + active]
            return carry

        lax.fori_loop(0, steps, advance, 0)
        for q in range(0, active, 8):
            upper, lower = split(half[:, q : q + 8, :width].reshape(rows * 8, width))
            hi, lo = wide_hi[8 * q :, :], wide_lo[8 * q :, :]
            both = dot(jnp.concatenate([hi, lo], axis=0), upper)
            part = both[: 8 * (active - q)] + both[8 * (active - q) :] + dot(hi, lower)
            square[q:, q : q + 8, :width] = part.reshape(active - q, 8, width)
        for p in range(active):
            target[p * (p + 1) // 2 : (p + 1) * (p + 2) // 2, :] = square[p, : p + 1, :width]

    turned = flat[...].T[:, :pairs]
    first = (index_mu & 1) == 0
    for i in range(8):
        a, b = turned[32 * i : 32 * i + 16], turned[32 * i + 16 : 32 * i + 32]
        keep[16 * i : 16 * i + 16, :] = jnp.where(first, a, b)
        give[16 * i : 16 * i + 16, :] = jnp.where(first, b, a)


def turn(me, turned_orbitals, vectors, columns):
    rows, cols, depth = vectors.shape
    count = columns.shape[2]
    active = turned_orbitals.shape[0]
    pairs = active * (active + 1) // 2
    steps = 8
    return pl.pallas_call(
        turn_kernel,
        out_shape=(
            jax.ShapeDtypeStruct((pairs, depth), f32),
            jax.ShapeDtypeStruct((count // 2, pairs), f32),
            jax.ShapeDtypeStruct((count // 2, pairs), f32),
        ),
        in_specs=[smem, vmem, hbm, hbm],
        out_specs=(vmem,) * 3,
        scratch_shapes=[
            pltpu.VMEM(vectors.shape, f32),
            pltpu.VMEM(columns.shape, f32),
            pltpu.VMEM((active * 8, rows * 8), bf16),
            pltpu.VMEM((active * 8, rows * 8), bf16),
            pltpu.VMEM((96, 2 * cols), bf16),
            pltpu.VMEM((rows, active, depth), f32),
            pltpu.VMEM((active, active, depth), f32),
            pltpu.VMEM((pl.cdiv(pairs, LANES) * LANES, count), f32),
            pltpu.SemaphoreType.DMA((2, steps)),
        ],
        compiler_params=params(56),
        cost_estimate=pl.CostEstimate(
            flops=10**10, bytes_accessed=4 * (vectors.size + columns.size), transcendentals=0
        ),
        name="turn",
    )(me, turned_orbitals, vectors, columns)


def choose_kernel(
    me, near_hot, far_hot, near, far, upper_v, lower_v, mine_c, got_c, part, rows_out, scale_out, rows_all, scaling, keep_hi, keep_lo, sems
):
    slots, width = near.shape
    depth = width - LANES
    count = near_hot.shape[0]
    core = (me[0] >> 3) & 1
    near_hi, near_lo = split(near[...])
    far_hi, far_lo = split(far[...])
    hi = dot(near_hot[...], near_hi) + dot(far_hot[...], far_hi)
    lo = dot(near_hot[...], near_lo) + dot(far_hot[...], far_lo)
    hi16, lo16 = hi.astype(bf16), lo.astype(bf16)
    rows_all[:count, :] = hi16[:, :depth]
    rows_all[count:, :] = lo16[:, :depth]
    scaling[...] = (hi[:, depth:] + lo[:, depth:]).T[:8]
    copies = [
        pltpu.make_async_copy(rows_all, rows_out, sems.at[0]),
        pltpu.make_async_copy(scaling, scale_out, sems.at[1]),
    ]
    for copy in copies:
        copy.start()
    keep_hi[...] = hi16.reshape(keep_hi.shape)
    keep_lo[...] = lo16.reshape(keep_lo.shape)
    home_hi = keep_hi[:, core].reshape(-1, width)
    home_lo = keep_lo[:, core].reshape(-1, width)
    moved = (
        dot_nt(home_hi[:, :depth], upper_v[...])
        + dot_nt(home_lo[:, :depth], upper_v[...])
        + dot_nt(home_hi[:, :depth], lower_v[...])
    )
    scale = home_hi[:, depth : depth + 1].astype(f32) + home_lo[:, depth : depth + 1].astype(f32)
    part[...] = ((mine_c[...] + got_c[...] - moved) * scale).reshape(part.shape)
    for copy in copies:
        copy.wait()


def choose(me, near_hot, far_hot, near, far, upper_v, lower_v, mine_c, got_c):
    count, slots = near_hot.shape
    width = near.shape[1]
    depth = width - LANES
    pairs = upper_v.shape[0]
    return pl.pallas_call(
        choose_kernel,
        out_shape=(
            jax.ShapeDtypeStruct((64, count // 128, pairs), f32),
            pltpu.HBM((2 * count, depth), bf16),
            pltpu.HBM((8, count), f32),
        ),
        in_specs=[smem] + [vmem] * 8,
        out_specs=(vmem, pl.BlockSpec(memory_space=pltpu.HBM), pl.BlockSpec(memory_space=pltpu.HBM)),
        scratch_shapes=[
            pltpu.VMEM((2 * count, depth), bf16),
            pltpu.VMEM((8, count), f32),
            pltpu.VMEM((8, 2, 16, width), bf16),
            pltpu.VMEM((8, 2, 16, width), bf16),
            pltpu.SemaphoreType.DMA((2,)),
        ],
        compiler_params=params(24),
        cost_estimate=pl.CostEstimate(flops=2 * 10**9, bytes_accessed=6 * 10**6, transcendentals=0),
        name="choose",
    )(me, near_hot, far_hot, near, far, upper_v, lower_v, mine_c, got_c)


def update_kernel(vectors, columns, diagonal, rows_all, scaling, out, block, beside, sems):
    rows, cols, depth = block.shape
    count = beside.shape[2]
    steps = sems.shape[1]
    tall = rows // steps

    def fetch(step):
        part = pl.ds(step * tall, tall)
        return (
            pltpu.make_async_copy(vectors.at[part], block.at[part], sems.at[0, step]),
            pltpu.make_async_copy(columns.at[part], beside.at[part], sems.at[1, step]),
        )

    for step in range(steps):
        for copy in fetch(step):
            copy.start()

    def advance(step, carry):
        for copy in fetch(step):
            copy.wait()
        part = pl.ds(pl.multiple_of(step * tall, tall), tall)
        upper, lower = split(block[part].reshape(tall * cols, depth))
        both = dot_nt(upper, rows_all[...])
        update = both[:, :count] + both[:, count:] + dot_nt(lower, rows_all[:count, :])
        fresh = (beside[part].reshape(tall * cols, count) - update) * scaling[:1, :]
        square = fresh * fresh
        folded = (square[:, :LANES] + square[:, LANES:]).reshape(tall, cols, LANES)
        out[part, :] = diagonal[part, :] - jnp.sum(jnp.swapaxes(folded, 1, 2), axis=1)
        return carry

    lax.fori_loop(0, steps, advance, 0)


def update(vectors, columns, diagonal, rows_all, scaling):
    rows, cols, depth = vectors.shape
    count = columns.shape[2]
    steps = 8
    return pl.pallas_call(
        update_kernel,
        out_shape=jax.ShapeDtypeStruct((rows, cols), f32),
        in_specs=[hbm, hbm, vmem, vmem, vmem],
        out_specs=vmem,
        scratch_shapes=[
            pltpu.VMEM(vectors.shape, f32),
            pltpu.VMEM(columns.shape, f32),
            pltpu.SemaphoreType.DMA((2, steps)),
        ],
        compiler_params=params(56),
        cost_estimate=pl.CostEstimate(
            flops=6 * rows * cols * depth * count, bytes_accessed=4 * (vectors.size + columns.size), transcendentals=0
        ),
        name="update",
    )(vectors, columns, diagonal, rows_all, scaling)


def local(vectors, columns, diagonal, orbitals, pivots):
    depth = vectors.shape[2]
    count = pivots.shape[0]
    core = lax.axis_index("c")
    me = lax.axis_index(("y", "zh", "c", "zl", "x")).reshape(1)
    near = exchange(pick(me, pivots, diagonal, vectors), PEERS)

    own_chip, own_core = (pivots >> 17) * 8 + ((pivots & 1023) >> 7), (pivots >> 16) & 1
    block = own_chip * 2 + own_core
    order = jnp.arange(count)
    rank = jnp.sum((block[None, :] == block[:, None]) & (order[None, :] < order[:, None]), axis=1)
    place = jnp.where(own_core == core, own_chip * SLOTS + rank, -1)
    other = jnp.where(own_core == core, -1, own_chip * SLOTS + rank)
    slot = jnp.arange(64 * SLOTS)
    near_hot = (place[:, None] == slot[None, :]).astype(bf16)
    far_hot = (other[:, None] == slot[None, :]).astype(bf16)

    mine_v, keep_c, give_c = turn(me, orbitals.T, vectors, columns)
    got_v, got_c = sibling(mine_v), sibling(give_c)
    chip_v = mine_v + got_v
    upper_v = lax.reduce_precision(chip_v, 8, 7)
    lower_v = (chip_v - upper_v).astype(bf16)
    upper_v = upper_v.astype(bf16)

    near, keep_c = lax.optimization_barrier((near, keep_c))
    far = sibling(near)
    flat = (64 * SLOTS, depth + LANES)
    part, rows_all, scaling = choose(
        me, near_hot, far_hot, near.reshape(flat), far.reshape(flat), upper_v, lower_v, keep_c, got_c
    )
    arrived = exchange(part, PEERS)
    updated = update(vectors, columns, diagonal, rows_all, scaling)
    return arrived.sum(axis=0), updated


def solution(mesh):
    fine = Mesh(mesh.devices.reshape(4, 2, 2, 2, 4), ("y", "zh", "c", "zl", "x"))
    mu, nu = ("y", "zh", "c"), ("zl", "x")
    placed = (P(mu, nu, None), P(mu, nu, None), P(mu, nu), P(), P())
    return jax.shard_map(
        local,
        mesh=fine,
        in_specs=placed,
        out_specs=(P(mu + nu, None), P(mu, nu)),
        check_vma=False,
    )
```

```python
import functools

import jax
import jax.numpy as jnp
from jax import lax
from jax.experimental import pallas as pl
from jax.experimental.pallas import tpu as pltpu
from jax.sharding import Mesh, PartitionSpec as P

SLOTS = 8
PER_ROW = 4
LANES = 128
PEERS = ("y", "zh", "zl", "x")
f32, bf16 = jnp.float32, jnp.bfloat16
smem = pl.BlockSpec(memory_space=pltpu.SMEM)
vmem = pl.BlockSpec(memory_space=pltpu.VMEM)
hbm = pl.BlockSpec(memory_space=pl.ANY)


def exchange(value, axes):
    return lax.all_to_all(value, axes, split_axis=0, concat_axis=0, tiled=True)


def sibling(value):
    return lax.ppermute(value, "c", [(0, 1), (1, 0)])


def iota(shape, dim):
    return lax.broadcasted_iota(jnp.int32, shape, dim)


def split(value):
    upper = value.astype(bf16)
    return upper, (value - upper.astype(f32)).astype(bf16)


def dot(a, b):
    return jnp.dot(a, b, preferred_element_type=f32)


def dot_nt(a, b):
    return lax.dot_general(a, b, (((1,), (1,)), ((), ())), preferred_element_type=f32)


def params(mib):
    return pltpu.CompilerParams(vmem_limit_bytes=mib << 20)


def pick_kernel(me, pivots, diagonal, vectors, out, rows, spots, tile, index, sems):
    count = pivots.shape[0]
    depth = vectors.shape[2]
    for slot in range(2 * SLOTS):
        index[slot] = 0
    key = (me[0] >> 3) * 65536 + (me[0] & 7) * LANES
    group = 16

    def scan(i, found):
        pairs = [pivots[i * group + j] for j in range(group)]
        owned = [((pair & 0xF0380) == key).astype(jnp.int32) for pair in pairs]

        def note(spot):
            for pair, own in zip(pairs, owned):
                index[spot] = pair
                spot = spot + own
            return spot

        total = functools.reduce(lambda a, b: a | b, owned)
        return lax.cond(total > 0, note, lambda spot: spot, found)

    found = lax.fori_loop(0, count // group, scan, 0)
    copies = []
    for slot in range(SLOTS):
        row, col = (index[slot] >> 10) & 63, index[slot] & 127
        here = pl.ds(slot, 1)
        copies.append(pltpu.make_async_copy(vectors.at[row, pl.ds(col, 1), :], rows.at[here, :], sems.at[0, slot]))
        copies.append(pltpu.make_async_copy(diagonal.at[pl.ds(row, 1), :], spots.at[here, :], sems.at[1, slot]))
    for copy in copies:
        copy.start()
    column = iota((SLOTS, 1), 0)
    chosen = jnp.zeros((SLOTS, 1), jnp.int32)
    for slot in range(SLOTS):
        chosen = jnp.where(column == slot, index[slot] & 127, chosen)
    for copy in copies:
        copy.wait()
    used = iota((SLOTS, 1), 0) < found
    picked = jnp.where(used, rows[...], 0.0)
    residual = jnp.sum(jnp.where(iota((SLOTS, LANES), 1) == chosen, spots[...], 0.0), axis=1, keepdims=True) - jnp.sum(picked * picked, axis=1, keepdims=True)
    scale = lax.rsqrt(jnp.maximum(jnp.where(used, residual, 1.0), 1.0))
    lane = iota((1, LANES), 1) // (LANES // PER_ROW)
    for r in range(SLOTS // PER_ROW):
        line = jnp.zeros((1, LANES), f32)
        for i in range(PER_ROW):
            slot = r * PER_ROW + i
            tile[r : r + 1, depth * i : depth * (i + 1)] = picked[slot : slot + 1, :]
            line = jnp.where(lane == i, scale[slot : slot + 1, :], line)
        tile[r : r + 1, depth * PER_ROW :] = line
    out[...] = jnp.broadcast_to(tile[...][None], out.shape)


def pick(me, pivots, diagonal, vectors):
    depth = vectors.shape[2]
    return pl.pallas_call(
        pick_kernel,
        out_shape=jax.ShapeDtypeStruct((64, SLOTS // PER_ROW, depth * PER_ROW + LANES), f32),
        in_specs=[smem, smem, hbm, hbm],
        out_specs=vmem,
        scratch_shapes=[
            pltpu.VMEM((SLOTS, depth), f32),
            pltpu.VMEM((SLOTS, LANES), f32),
            pltpu.VMEM((SLOTS // PER_ROW, depth * PER_ROW + LANES), f32),
            pltpu.SMEM((2 * SLOTS,), jnp.int32),
            pltpu.SemaphoreType.DMA((2, SLOTS)),
        ],
        name="pick",
    )(me, pivots, diagonal, vectors)


def turn_kernel(
    me, turned_orbitals, vectors, columns, out, keep, give, block, beside, wide_hi, wide_lo, right2, half, square, flat, sems
):
    rows, cols, _ = block.shape
    active, pairs = turned_orbitals.shape[0], out.shape[0]
    steps = sems.shape[1]
    tall = rows // steps

    def fetch(kind, step):
        part = pl.ds(step * tall, tall)
        source, target = ((vectors, block), (columns, beside))[kind]
        return pltpu.make_async_copy(source.at[part], target.at[part], sems.at[kind, step])

    for kind in range(2):
        for step in range(steps):
            fetch(kind, step).start()

    index_mu = me[0] >> 3
    left = turned_orbitals[:, pl.ds(pl.multiple_of((index_mu >> 1) * LANES, LANES), LANES)]
    right = turned_orbitals[:, pl.ds(pl.multiple_of((me[0] & 7) * cols, cols), cols)]
    high = (active * 8, active)
    spread_rows = jnp.where(iota(high, 0) // 8 == iota(high, 1), 1.0, 0.0).astype(bf16)
    long = (LANES, rows * 8)
    spread_cols = jnp.where(iota(long, 0) == iota(long, 1) // 8 + (index_mu & 1) * rows, 1.0, 0.0).astype(bf16)
    full = (active * 8, rows * 8)
    same = iota(full, 0) % 8 == iota(full, 1) % 8
    for part, wide in zip(split(left), (wide_hi, wide_lo)):
        repeated = dot(dot(spread_rows, part).astype(bf16), spread_cols)
        wide[...] = jnp.where(same, repeated, 0.0).astype(bf16)
    eye = jnp.where(iota((48, active), 0) == iota((48, active), 1), 1.0, 0.0).astype(bf16)
    upper, lower = [dot(eye, part).astype(bf16) for part in split(right)]
    right2[:48, :cols] = upper
    right2[:48, cols:] = upper
    right2[48:, :cols] = lower
    right2[48:, cols:] = jnp.zeros_like(lower)

    for kind, (value, target) in enumerate(((block, out), (beside, flat))):
        width = value.shape[2]

        def advance(step, carry):
            fetch(kind, step).wait()
            for i in range(tall):
                row = step * tall + i
                both = dot(right2[...], jnp.concatenate(split(value[row]), axis=0))
                half[row, :, :width] = both[:active] + both[48 : 48 + active]
            return carry

        lax.fori_loop(0, steps, advance, 0)
        for q in range(0, active, 8):
            upper, lower = split(half[:, q : q + 8, :width].reshape(rows * 8, width))
            hi, lo = wide_hi[8 * q :, :], wide_lo[8 * q :, :]
            both = dot(jnp.concatenate([hi, lo], axis=0), upper)
            part = both[: 8 * (active - q)] + both[8 * (active - q) :] + dot(hi, lower)
            square[q:, q : q + 8, :width] = part.reshape(active - q, 8, width)
        for p in range(active):
            target[p * (p + 1) // 2 : (p + 1) * (p + 2) // 2, :] = square[p, : p + 1, :width]

    turned = flat[...].T[:, :pairs]
    first = (index_mu & 1) == 0
    for i in range(8):
        a, b = turned[32 * i : 32 * i + 16], turned[32 * i + 16 : 32 * i + 32]
        keep[16 * i : 16 * i + 16, :] = jnp.where(first, a, b)
        give[16 * i : 16 * i + 16, :] = jnp.where(first, b, a)


def turn(me, turned_orbitals, vectors, columns):
    rows, cols, depth = vectors.shape
    count = columns.shape[2]
    active = turned_orbitals.shape[0]
    pairs = active * (active + 1) // 2
    steps = 8
    return pl.pallas_call(
        turn_kernel,
        out_shape=(
            jax.ShapeDtypeStruct((pairs, depth), f32),
            jax.ShapeDtypeStruct((count // 2, pairs), f32),
            jax.ShapeDtypeStruct((count // 2, pairs), f32),
        ),
        in_specs=[smem, vmem, hbm, hbm],
        out_specs=(vmem,) * 3,
        scratch_shapes=[
            pltpu.VMEM(vectors.shape, f32),
            pltpu.VMEM(columns.shape, f32),
            pltpu.VMEM((active * 8, rows * 8), bf16),
            pltpu.VMEM((active * 8, rows * 8), bf16),
            pltpu.VMEM((96, 2 * cols), bf16),
            pltpu.VMEM((rows, active, depth), f32),
            pltpu.VMEM((active, active, depth), f32),
            pltpu.VMEM((pl.cdiv(pairs, LANES) * LANES, count), f32),
            pltpu.SemaphoreType.DMA((2, steps)),
        ],
        compiler_params=params(56),
        cost_estimate=pl.CostEstimate(
            flops=10**10, bytes_accessed=4 * (vectors.size + columns.size), transcendentals=0
        ),
        name="turn",
    )(me, turned_orbitals, vectors, columns)


def unpack(packed):
    rows = packed.shape[0] * packed.shape[1]
    depth = (packed.shape[2] - LANES) // PER_ROW
    flat = packed[...].reshape(rows, packed.shape[2])
    vectors = [flat[:, depth * i : depth * (i + 1)] for i in range(PER_ROW)]
    spots = [depth * PER_ROW + LANES // PER_ROW * i for i in range(PER_ROW)]
    scales = [jnp.broadcast_to(flat[:, spot : spot + 1], (rows, LANES)) for spot in spots]
    return jnp.concatenate([jnp.concatenate(vectors, axis=0), jnp.concatenate(scales, axis=0)], axis=1)


def choose_kernel(
    me, near_hot, far_hot, near, far, upper_v, lower_v, mine_c, got_c, part, rows_out, scale_out, rows_all, scaling, keep_hi, keep_lo, sems
):
    depth = rows_all.shape[1]
    width = depth + LANES
    count = near_hot.shape[0]
    core = (me[0] >> 3) & 1
    near_hi, near_lo = split(unpack(near))
    far_hi, far_lo = split(unpack(far))
    hi = dot(near_hot[...], near_hi) + dot(far_hot[...], far_hi)
    lo = dot(near_hot[...], near_lo) + dot(far_hot[...], far_lo)
    hi16, lo16 = hi.astype(bf16), lo.astype(bf16)
    rows_all[:count, :] = hi16[:, :depth]
    rows_all[count:, :] = lo16[:, :depth]
    scaling[...] = (hi[:, depth:] + lo[:, depth:]).T[:8]
    copies = [
        pltpu.make_async_copy(rows_all, rows_out, sems.at[0]),
        pltpu.make_async_copy(scaling, scale_out, sems.at[1]),
    ]
    for copy in copies:
        copy.start()
    keep_hi[...] = hi16.reshape(keep_hi.shape)
    keep_lo[...] = lo16.reshape(keep_lo.shape)
    home_hi = keep_hi[:, core].reshape(-1, width)
    home_lo = keep_lo[:, core].reshape(-1, width)
    moved = (
        dot_nt(home_hi[:, :depth], upper_v[...])
        + dot_nt(home_lo[:, :depth], upper_v[...])
        + dot_nt(home_hi[:, :depth], lower_v[...])
    )
    scale = home_hi[:, depth : depth + 1].astype(f32) + home_lo[:, depth : depth + 1].astype(f32)
    part[...] = ((mine_c[...] + got_c[...] - moved) * scale).reshape(part.shape)
    for copy in copies:
        copy.wait()


def choose(me, near_hot, far_hot, near, far, upper_v, lower_v, mine_c, got_c):
    count, slots = near_hot.shape
    depth = upper_v.shape[1]
    width = depth + LANES
    pairs = upper_v.shape[0]
    return pl.pallas_call(
        choose_kernel,
        out_shape=(
            jax.ShapeDtypeStruct((64, count // 128, pairs), f32),
            pltpu.HBM((2 * count, depth), bf16),
            pltpu.HBM((8, count), f32),
        ),
        in_specs=[smem] + [vmem] * 8,
        out_specs=(vmem, pl.BlockSpec(memory_space=pltpu.HBM), pl.BlockSpec(memory_space=pltpu.HBM)),
        scratch_shapes=[
            pltpu.VMEM((2 * count, depth), bf16),
            pltpu.VMEM((8, count), f32),
            pltpu.VMEM((8, 2, 16, width), bf16),
            pltpu.VMEM((8, 2, 16, width), bf16),
            pltpu.SemaphoreType.DMA((2,)),
        ],
        compiler_params=params(24),
        cost_estimate=pl.CostEstimate(flops=2 * 10**9, bytes_accessed=6 * 10**6, transcendentals=0),
        name="choose",
    )(me, near_hot, far_hot, near, far, upper_v, lower_v, mine_c, got_c)


def update_kernel(vectors, columns, diagonal, rows_all, scaling, out, block, beside, sems):
    rows, cols, depth = block.shape
    count = beside.shape[2]
    steps = sems.shape[1]
    tall = rows // steps

    def fetch(step):
        part = pl.ds(step * tall, tall)
        return (
            pltpu.make_async_copy(vectors.at[part], block.at[part], sems.at[0, step]),
            pltpu.make_async_copy(columns.at[part], beside.at[part], sems.at[1, step]),
        )

    for step in range(steps):
        for copy in fetch(step):
            copy.start()

    def advance(step, carry):
        for copy in fetch(step):
            copy.wait()
        part = pl.ds(pl.multiple_of(step * tall, tall), tall)
        upper, lower = split(block[part].reshape(tall * cols, depth))
        both = dot_nt(upper, rows_all[...])
        update = both[:, :count] + both[:, count:] + dot_nt(lower, rows_all[:count, :])
        fresh = (beside[part].reshape(tall * cols, count) - update) * scaling[:1, :]
        square = fresh * fresh
        folded = (square[:, :LANES] + square[:, LANES:]).reshape(tall, cols, LANES)
        out[part, :] = diagonal[part, :] - jnp.sum(jnp.swapaxes(folded, 1, 2), axis=1)
        return carry

    lax.fori_loop(0, steps, advance, 0)


def update(vectors, columns, diagonal, rows_all, scaling):
    rows, cols, depth = vectors.shape
    count = columns.shape[2]
    steps = 8
    return pl.pallas_call(
        update_kernel,
        out_shape=jax.ShapeDtypeStruct((rows, cols), f32),
        in_specs=[hbm, hbm, vmem, vmem, vmem],
        out_specs=vmem,
        scratch_shapes=[
            pltpu.VMEM(vectors.shape, f32),
            pltpu.VMEM(columns.shape, f32),
            pltpu.SemaphoreType.DMA((2, steps)),
        ],
        compiler_params=params(56),
        cost_estimate=pl.CostEstimate(
            flops=6 * rows * cols * depth * count, bytes_accessed=4 * (vectors.size + columns.size), transcendentals=0
        ),
        name="update",
    )(vectors, columns, diagonal, rows_all, scaling)


def local(vectors, columns, diagonal, orbitals, pivots):
    count = pivots.shape[0]
    core = lax.axis_index("c")
    me = lax.axis_index(("y", "zh", "c", "zl", "x")).reshape(1)
    near = exchange(pick(me, pivots, diagonal, vectors), PEERS)

    own_chip, own_core = (pivots >> 17) * 8 + ((pivots & 1023) >> 7), (pivots >> 16) & 1
    block = own_chip * 2 + own_core
    order = jnp.arange(count)
    rank = jnp.sum((block[None, :] == block[:, None]) & (order[None, :] < order[:, None]), axis=1)
    spot = rank % PER_ROW * (64 * SLOTS // PER_ROW) + own_chip * (SLOTS // PER_ROW) + rank // PER_ROW
    place = jnp.where(own_core == core, spot, -1)
    other = jnp.where(own_core == core, -1, spot)
    slot = jnp.arange(64 * SLOTS)
    near_hot = (place[:, None] == slot[None, :]).astype(bf16)
    far_hot = (other[:, None] == slot[None, :]).astype(bf16)

    mine_v, keep_c, give_c = turn(me, orbitals.T, vectors, columns)
    got_v, got_c = sibling(mine_v), sibling(give_c)
    chip_v = mine_v + got_v
    upper_v = lax.reduce_precision(chip_v, 8, 7)
    lower_v = (chip_v - upper_v).astype(bf16)
    upper_v = upper_v.astype(bf16)

    near, keep_c = lax.optimization_barrier((near, keep_c))
    far = sibling(near)
    part, rows_all, scaling = choose(me, near_hot, far_hot, near, far, upper_v, lower_v, keep_c, got_c)
    arrived = exchange(part, PEERS)
    updated = update(vectors, columns, diagonal, rows_all, scaling)
    return arrived.sum(axis=0), updated


def solution(mesh):
    fine = Mesh(mesh.devices.reshape(4, 2, 2, 2, 4), ("y", "zh", "c", "zl", "x"))
    mu, nu = ("y", "zh", "c"), ("zl", "x")
    placed = (P(mu, nu, None), P(mu, nu, None), P(mu, nu), P(), P())
    return jax.shard_map(
        local,
        mesh=fine,
        in_specs=placed,
        out_specs=(P(mu + nu, None), P(mu, nu)),
        check_vma=False,
    )
```

```python
import functools

import jax
import jax.numpy as jnp
from jax import lax
from jax.experimental import pallas as pl
from jax.experimental.pallas import tpu as pltpu
from jax.sharding import Mesh, PartitionSpec as P

SLOTS = 8
PER_ROW = 4
LANES = 128
PEERS = ("y", "zh", "zl", "x")
f32, bf16 = jnp.float32, jnp.bfloat16
smem = pl.BlockSpec(memory_space=pltpu.SMEM)
vmem = pl.BlockSpec(memory_space=pltpu.VMEM)
hbm = pl.BlockSpec(memory_space=pl.ANY)


def exchange(value, axes):
    return lax.all_to_all(value, axes, split_axis=0, concat_axis=0, tiled=True)


def sibling(value):
    return lax.ppermute(value, "c", [(0, 1), (1, 0)])


def iota(shape, dim):
    return lax.broadcasted_iota(jnp.int32, shape, dim)


def split(value):
    upper = value.astype(bf16)
    return upper, (value - upper.astype(f32)).astype(bf16)


def dot(a, b):
    return jnp.dot(a, b, preferred_element_type=f32)


def dot_nt(a, b):
    return lax.dot_general(a, b, (((1,), (1,)), ((), ())), preferred_element_type=f32)


def params(mib):
    return pltpu.CompilerParams(vmem_limit_bytes=mib << 20)


def pick_kernel(me, pivots, diagonal, vectors, out, rows, spots, tile, index, sems):
    count = pivots.shape[0]
    depth = vectors.shape[2]
    for slot in range(2 * SLOTS):
        index[slot] = 0
    key = (me[0] >> 3) * 65536 + (me[0] & 7) * LANES
    group = 16

    def scan(i, found):
        pairs = [pivots[i * group + j] for j in range(group)]
        owned = [((pair & 0xF0380) == key).astype(jnp.int32) for pair in pairs]

        def note(spot):
            for pair, own in zip(pairs, owned):
                index[spot] = pair
                spot = spot + own
            return spot

        total = functools.reduce(lambda a, b: a | b, owned)
        return lax.cond(total > 0, note, lambda spot: spot, found)

    found = lax.fori_loop(0, count // group, scan, 0)
    copies = []
    for slot in range(SLOTS):
        row, col = (index[slot] >> 10) & 63, index[slot] & 127
        here = pl.ds(slot, 1)
        copies.append(pltpu.make_async_copy(vectors.at[row, pl.ds(col, 1), :], rows.at[here, :], sems.at[0, slot]))
        copies.append(pltpu.make_async_copy(diagonal.at[pl.ds(row, 1), :], spots.at[here, :], sems.at[1, slot]))
    for copy in copies:
        copy.start()
    column = iota((SLOTS, 1), 0)
    chosen = jnp.zeros((SLOTS, 1), jnp.int32)
    for slot in range(SLOTS):
        chosen = jnp.where(column == slot, index[slot] & 127, chosen)
    for copy in copies:
        copy.wait()
    used = iota((SLOTS, 1), 0) < found
    picked = jnp.where(used, rows[...], 0.0)
    residual = jnp.sum(jnp.where(iota((SLOTS, LANES), 1) == chosen, spots[...], 0.0), axis=1, keepdims=True) - jnp.sum(picked * picked, axis=1, keepdims=True)
    scale = lax.rsqrt(jnp.maximum(jnp.where(used, residual, 1.0), 1.0))
    lane = iota((1, LANES), 1) // (LANES // PER_ROW)
    for r in range(SLOTS // PER_ROW):
        line = jnp.zeros((1, LANES), f32)
        for i in range(PER_ROW):
            slot = r * PER_ROW + i
            tile[r : r + 1, depth * i : depth * (i + 1)] = picked[slot : slot + 1, :]
            line = jnp.where(lane == i, scale[slot : slot + 1, :], line)
        tile[r : r + 1, depth * PER_ROW :] = line
    out[...] = jnp.broadcast_to(tile[...][None], out.shape)


def pick(me, pivots, diagonal, vectors):
    depth = vectors.shape[2]
    return pl.pallas_call(
        pick_kernel,
        out_shape=jax.ShapeDtypeStruct((64, SLOTS // PER_ROW, depth * PER_ROW + LANES), f32),
        in_specs=[smem, smem, hbm, hbm],
        out_specs=vmem,
        scratch_shapes=[
            pltpu.VMEM((SLOTS, depth), f32),
            pltpu.VMEM((SLOTS, LANES), f32),
            pltpu.VMEM((SLOTS // PER_ROW, depth * PER_ROW + LANES), f32),
            pltpu.SMEM((2 * SLOTS,), jnp.int32),
            pltpu.SemaphoreType.DMA((2, SLOTS)),
        ],
        name="pick",
    )(me, pivots, diagonal, vectors)


def turn_kernel(
    me, turned_orbitals, vectors, columns, out, keep, give, block, beside, wide_hi, wide_lo, right2, half, square, flat, sems
):
    rows, cols, _ = block.shape
    active, pairs = turned_orbitals.shape[0], out.shape[0]
    steps = sems.shape[1]
    tall = rows // steps

    def fetch(kind, step):
        part = pl.ds(step * tall, tall)
        source, target = ((vectors, block), (columns, beside))[kind]
        return pltpu.make_async_copy(source.at[part], target.at[part], sems.at[kind, step])

    for kind in range(2):
        for step in range(steps):
            fetch(kind, step).start()

    index_mu = me[0] >> 3
    left = turned_orbitals[:, pl.ds(pl.multiple_of((index_mu >> 1) * LANES, LANES), LANES)]
    right = turned_orbitals[:, pl.ds(pl.multiple_of((me[0] & 7) * cols, cols), cols)]
    high = (active * 8, active)
    spread_rows = jnp.where(iota(high, 0) // 8 == iota(high, 1), 1.0, 0.0).astype(bf16)
    long = (LANES, rows * 8)
    spread_cols = jnp.where(iota(long, 0) == iota(long, 1) // 8 + (index_mu & 1) * rows, 1.0, 0.0).astype(bf16)
    full = (active * 8, rows * 8)
    same = iota(full, 0) % 8 == iota(full, 1) % 8
    for part, wide in zip(split(left), (wide_hi, wide_lo)):
        repeated = dot(dot(spread_rows, part).astype(bf16), spread_cols)
        wide[...] = jnp.where(same, repeated, 0.0).astype(bf16)
    eye = jnp.where(iota((48, active), 0) == iota((48, active), 1), 1.0, 0.0).astype(bf16)
    upper, lower = [dot(eye, part).astype(bf16) for part in split(right)]
    right2[:48, :cols] = upper
    right2[:48, cols:] = upper
    right2[48:, :cols] = lower
    right2[48:, cols:] = jnp.zeros_like(lower)

    for kind, (value, target) in enumerate(((block, out), (beside, flat))):
        width = value.shape[2]

        def advance(step, carry):
            fetch(kind, step).wait()
            for i in range(tall):
                row = step * tall + i
                both = dot(right2[...], jnp.concatenate(split(value[row]), axis=0))
                half[row, :, :width] = both[:active] + both[48 : 48 + active]
            return carry

        lax.fori_loop(0, steps, advance, 0)
        for q in range(0, active, 8):
            upper, lower = split(half[:, q : q + 8, :width].reshape(rows * 8, width))
            hi, lo = wide_hi[8 * q :, :], wide_lo[8 * q :, :]
            both = dot(jnp.concatenate([hi, lo], axis=0), upper)
            part = both[: 8 * (active - q)] + both[8 * (active - q) :] + dot(hi, lower)
            square[q:, q : q + 8, :width] = part.reshape(active - q, 8, width)
        for p in range(active):
            target[p * (p + 1) // 2 : (p + 1) * (p + 2) // 2, :] = square[p, : p + 1, :width]

    turned = flat[...].T[:, :pairs]
    first = (index_mu & 1) == 0
    for i in range(8):
        a, b = turned[32 * i : 32 * i + 16], turned[32 * i + 16 : 32 * i + 32]
        keep[16 * i : 16 * i + 16, :] = jnp.where(first, a, b)
        give[16 * i : 16 * i + 16, :] = jnp.where(first, b, a)


def turn(me, turned_orbitals, vectors, columns):
    rows, cols, depth = vectors.shape
    count = columns.shape[2]
    active = turned_orbitals.shape[0]
    pairs = active * (active + 1) // 2
    steps = 8
    return pl.pallas_call(
        turn_kernel,
        out_shape=(
            jax.ShapeDtypeStruct((pairs, depth), f32),
            jax.ShapeDtypeStruct((count // 2, pairs), f32),
            jax.ShapeDtypeStruct((count // 2, pairs), f32),
        ),
        in_specs=[smem, vmem, hbm, hbm],
        out_specs=(vmem,) * 3,
        scratch_shapes=[
            pltpu.VMEM(vectors.shape, f32),
            pltpu.VMEM(columns.shape, f32),
            pltpu.VMEM((active * 8, rows * 8), bf16),
            pltpu.VMEM((active * 8, rows * 8), bf16),
            pltpu.VMEM((96, 2 * cols), bf16),
            pltpu.VMEM((rows, active, depth), f32),
            pltpu.VMEM((active, active, depth), f32),
            pltpu.VMEM((pl.cdiv(pairs, LANES) * LANES, count), f32),
            pltpu.SemaphoreType.DMA((2, steps)),
        ],
        compiler_params=params(56),
        cost_estimate=pl.CostEstimate(
            flops=10**10, bytes_accessed=4 * (vectors.size + columns.size), transcendentals=0
        ),
        name="turn",
    )(me, turned_orbitals, vectors, columns)


def unpack(packed):
    rows = packed.shape[0] * packed.shape[1]
    depth = (packed.shape[2] - LANES) // PER_ROW
    flat = packed[...].reshape(rows, packed.shape[2])
    vectors = [flat[:, depth * i : depth * (i + 1)] for i in range(PER_ROW)]
    spots = [depth * PER_ROW + LANES // PER_ROW * i for i in range(PER_ROW)]
    scales = [jnp.broadcast_to(flat[:, spot : spot + 1], (rows, LANES)) for spot in spots]
    return jnp.concatenate([jnp.concatenate(vectors, axis=0), jnp.concatenate(scales, axis=0)], axis=1)


def line_up_kernel(hot, near, out):
    upper, lower = split(unpack(near))
    out[...] = dot(hot[...], upper) + dot(hot[...], lower)


def line_up(hot, near):
    depth = (near.shape[2] - LANES) // PER_ROW
    return pl.pallas_call(
        line_up_kernel,
        out_shape=jax.ShapeDtypeStruct((hot.shape[0], depth + LANES), f32),
        in_specs=[vmem, vmem],
        out_specs=vmem,
        compiler_params=params(16),
        cost_estimate=pl.CostEstimate(flops=4 * 10**8, bytes_accessed=2 * 10**6, transcendentals=0),
        name="line_up",
    )(hot, near)


def choose_kernel(
    me, far_hot, lined, far, upper_v, lower_v, mine_c, got_c, part, rows_out, scale_out, rows_all, scaling, keep_hi, keep_lo, sems
):
    depth = rows_all.shape[1]
    width = depth + LANES
    count = far_hot.shape[0]
    core = (me[0] >> 3) & 1
    far_hi, far_lo = split(unpack(far))
    rows = lined[...] + (dot(far_hot[...], far_hi) + dot(far_hot[...], far_lo))
    hi16, lo16 = split(rows)
    rows_all[:count, :] = hi16[:, :depth]
    rows_all[count:, :] = lo16[:, :depth]
    scaling[...] = rows[:, depth:].T[:8]
    copies = [
        pltpu.make_async_copy(rows_all, rows_out, sems.at[0]),
        pltpu.make_async_copy(scaling, scale_out, sems.at[1]),
    ]
    for copy in copies:
        copy.start()
    keep_hi[...] = hi16.reshape(keep_hi.shape)
    keep_lo[...] = lo16.reshape(keep_lo.shape)
    home_hi = keep_hi[:, core].reshape(-1, width)
    home_lo = keep_lo[:, core].reshape(-1, width)
    moved = (
        dot_nt(home_hi[:, :depth], upper_v[...])
        + dot_nt(home_lo[:, :depth], upper_v[...])
        + dot_nt(home_hi[:, :depth], lower_v[...])
    )
    scale = home_hi[:, depth : depth + 1].astype(f32) + home_lo[:, depth : depth + 1].astype(f32)
    part[...] = ((mine_c[...] + got_c[...] - moved) * scale).reshape(part.shape)
    for copy in copies:
        copy.wait()


def choose(me, far_hot, lined, far, upper_v, lower_v, mine_c, got_c):
    count = far_hot.shape[0]
    depth = upper_v.shape[1]
    width = depth + LANES
    pairs = upper_v.shape[0]
    return pl.pallas_call(
        choose_kernel,
        out_shape=(
            jax.ShapeDtypeStruct((64, count // 128, pairs), f32),
            pltpu.HBM((2 * count, depth), bf16),
            pltpu.HBM((8, count), f32),
        ),
        in_specs=[smem] + [vmem] * 7,
        out_specs=(vmem, pl.BlockSpec(memory_space=pltpu.HBM), pl.BlockSpec(memory_space=pltpu.HBM)),
        scratch_shapes=[
            pltpu.VMEM((2 * count, depth), bf16),
            pltpu.VMEM((8, count), f32),
            pltpu.VMEM((8, 2, 16, width), bf16),
            pltpu.VMEM((8, 2, 16, width), bf16),
            pltpu.SemaphoreType.DMA((2,)),
        ],
        compiler_params=params(24),
        cost_estimate=pl.CostEstimate(flops=2 * 10**9, bytes_accessed=6 * 10**6, transcendentals=0),
        name="choose",
    )(me, far_hot, lined, far, upper_v, lower_v, mine_c, got_c)


def update_kernel(vectors, columns, diagonal, rows_all, scaling, out, block, beside, sems):
    rows, cols, depth = block.shape
    count = beside.shape[2]
    steps = sems.shape[1]
    tall = rows // steps

    def fetch(step):
        part = pl.ds(step * tall, tall)
        return (
            pltpu.make_async_copy(vectors.at[part], block.at[part], sems.at[0, step]),
            pltpu.make_async_copy(columns.at[part], beside.at[part], sems.at[1, step]),
        )

    for step in range(steps):
        for copy in fetch(step):
            copy.start()

    def advance(step, carry):
        for copy in fetch(step):
            copy.wait()
        part = pl.ds(pl.multiple_of(step * tall, tall), tall)
        upper, lower = split(block[part].reshape(tall * cols, depth))
        both = dot_nt(upper, rows_all[...])
        update = both[:, :count] + both[:, count:] + dot_nt(lower, rows_all[:count, :])
        fresh = (beside[part].reshape(tall * cols, count) - update) * scaling[:1, :]
        square = fresh * fresh
        folded = (square[:, :LANES] + square[:, LANES:]).reshape(tall, cols, LANES)
        out[part, :] = diagonal[part, :] - jnp.sum(jnp.swapaxes(folded, 1, 2), axis=1)
        return carry

    lax.fori_loop(0, steps, advance, 0)


def update(vectors, columns, diagonal, rows_all, scaling):
    rows, cols, depth = vectors.shape
    count = columns.shape[2]
    steps = 8
    return pl.pallas_call(
        update_kernel,
        out_shape=jax.ShapeDtypeStruct((rows, cols), f32),
        in_specs=[hbm, hbm, vmem, vmem, vmem],
        out_specs=vmem,
        scratch_shapes=[
            pltpu.VMEM(vectors.shape, f32),
            pltpu.VMEM(columns.shape, f32),
            pltpu.SemaphoreType.DMA((2, steps)),
        ],
        compiler_params=params(56),
        cost_estimate=pl.CostEstimate(
            flops=6 * rows * cols * depth * count, bytes_accessed=4 * (vectors.size + columns.size), transcendentals=0
        ),
        name="update",
    )(vectors, columns, diagonal, rows_all, scaling)


def local(vectors, columns, diagonal, orbitals, pivots):
    count = pivots.shape[0]
    core = lax.axis_index("c")
    me = lax.axis_index(("y", "zh", "c", "zl", "x")).reshape(1)
    near = exchange(pick(me, pivots, diagonal, vectors), PEERS)

    own_chip, own_core = (pivots >> 17) * 8 + ((pivots & 1023) >> 7), (pivots >> 16) & 1
    block = own_chip * 2 + own_core
    order = jnp.arange(count)
    rank = jnp.sum((block[None, :] == block[:, None]) & (order[None, :] < order[:, None]), axis=1)
    spot = rank % PER_ROW * (64 * SLOTS // PER_ROW) + own_chip * (SLOTS // PER_ROW) + rank // PER_ROW
    place = jnp.where(own_core == core, spot, -1)
    other = jnp.where(own_core == core, -1, spot)
    slot = jnp.arange(64 * SLOTS)
    near_hot = (place[:, None] == slot[None, :]).astype(bf16)
    far_hot = (other[:, None] == slot[None, :]).astype(bf16)

    mine_v, keep_c, give_c = turn(me, orbitals.T, vectors, columns)
    got_v, got_c = sibling(mine_v), sibling(give_c)
    chip_v = mine_v + got_v
    upper_v = lax.reduce_precision(chip_v, 8, 7)
    lower_v = (chip_v - upper_v).astype(bf16)
    upper_v = upper_v.astype(bf16)

    near, keep_c = lax.optimization_barrier((near, keep_c))
    far = sibling(near)
    part, rows_all, scaling = choose(me, far_hot, line_up(near_hot, near), far, upper_v, lower_v, keep_c, got_c)
    arrived = exchange(part, PEERS)
    updated = update(vectors, columns, diagonal, rows_all, scaling)
    return arrived.sum(axis=0), updated


def solution(mesh):
    fine = Mesh(mesh.devices.reshape(4, 2, 2, 2, 4), ("y", "zh", "c", "zl", "x"))
    mu, nu = ("y", "zh", "c"), ("zl", "x")
    placed = (P(mu, nu, None), P(mu, nu, None), P(mu, nu), P(), P())
    return jax.shard_map(
        local,
        mesh=fine,
        in_specs=placed,
        out_specs=(P(mu + nu, None), P(mu, nu)),
        check_vma=False,
    )
```

```python
import functools

import jax
import jax.numpy as jnp
from jax import lax
from jax.experimental import pallas as pl
from jax.experimental.pallas import tpu as pltpu
from jax.sharding import Mesh, PartitionSpec as P

SLOTS = 8
PER_ROW = 4
LANES = 128
PEERS = ("y", "zh", "zl", "x")
f32, bf16 = jnp.float32, jnp.bfloat16
smem = pl.BlockSpec(memory_space=pltpu.SMEM)
vmem = pl.BlockSpec(memory_space=pltpu.VMEM)
hbm = pl.BlockSpec(memory_space=pl.ANY)


def exchange(value, axes):
    return lax.all_to_all(value, axes, split_axis=0, concat_axis=0, tiled=True)


def sibling(value):
    return lax.ppermute(value, "c", [(0, 1), (1, 0)])


def iota(shape, dim):
    return lax.broadcasted_iota(jnp.int32, shape, dim)


def split(value):
    upper = value.astype(bf16)
    return upper, (value - upper.astype(f32)).astype(bf16)


def dot(a, b):
    return jnp.dot(a, b, preferred_element_type=f32)


def dot_nt(a, b):
    return lax.dot_general(a, b, (((1,), (1,)), ((), ())), preferred_element_type=f32)


def params(mib):
    return pltpu.CompilerParams(vmem_limit_bytes=mib << 20)


def pick_kernel(me, pivots, diagonal, vectors, out, rows, spots, tile, index, sems):
    count = pivots.shape[0]
    depth = vectors.shape[2]
    for slot in range(2 * SLOTS):
        index[slot] = 0
    key = (me[0] >> 3) * 65536 + (me[0] & 7) * LANES
    group = 16

    def scan(i, found):
        pairs = [pivots[i * group + j] for j in range(group)]
        owned = [((pair & 0xF0380) == key).astype(jnp.int32) for pair in pairs]

        def note(spot):
            for pair, own in zip(pairs, owned):
                index[spot] = pair
                spot = spot + own
            return spot

        total = functools.reduce(lambda a, b: a | b, owned)
        return lax.cond(total > 0, note, lambda spot: spot, found)

    found = lax.fori_loop(0, count // group, scan, 0)
    copies = []
    for slot in range(SLOTS):
        row, col = (index[slot] >> 10) & 63, index[slot] & 127
        here = pl.ds(slot, 1)
        copies.append(pltpu.make_async_copy(vectors.at[row, pl.ds(col, 1), :], rows.at[here, :], sems.at[0, slot]))
        copies.append(pltpu.make_async_copy(diagonal.at[pl.ds(row, 1), :], spots.at[here, :], sems.at[1, slot]))
    for copy in copies:
        copy.start()
    column = iota((SLOTS, 1), 0)
    chosen = jnp.zeros((SLOTS, 1), jnp.int32)
    for slot in range(SLOTS):
        chosen = jnp.where(column == slot, index[slot] & 127, chosen)
    for copy in copies:
        copy.wait()
    used = iota((SLOTS, 1), 0) < found
    picked = jnp.where(used, rows[...], 0.0)
    residual = jnp.sum(jnp.where(iota((SLOTS, LANES), 1) == chosen, spots[...], 0.0), axis=1, keepdims=True) - jnp.sum(picked * picked, axis=1, keepdims=True)
    scale = lax.rsqrt(jnp.maximum(jnp.where(used, residual, 1.0), 1.0))
    lane = iota((1, LANES), 1) // (LANES // PER_ROW)
    for r in range(SLOTS // PER_ROW):
        line = jnp.zeros((1, LANES), f32)
        for i in range(PER_ROW):
            slot = r * PER_ROW + i
            tile[r : r + 1, depth * i : depth * (i + 1)] = picked[slot : slot + 1, :]
            line = jnp.where(lane == i, scale[slot : slot + 1, :], line)
        tile[r : r + 1, depth * PER_ROW :] = line
    out[...] = jnp.broadcast_to(tile[...][None], out.shape)


def pick(me, pivots, diagonal, vectors):
    depth = vectors.shape[2]
    return pl.pallas_call(
        pick_kernel,
        out_shape=jax.ShapeDtypeStruct((64, SLOTS // PER_ROW, depth * PER_ROW + LANES), f32),
        in_specs=[smem, smem, hbm, hbm],
        out_specs=vmem,
        scratch_shapes=[
            pltpu.VMEM((SLOTS, depth), f32),
            pltpu.VMEM((SLOTS, LANES), f32),
            pltpu.VMEM((SLOTS // PER_ROW, depth * PER_ROW + LANES), f32),
            pltpu.SMEM((2 * SLOTS,), jnp.int32),
            pltpu.SemaphoreType.DMA((2, SLOTS)),
        ],
        name="pick",
    )(me, pivots, diagonal, vectors)


def turn_kernel(
    me, turned_orbitals, vectors, columns, out, keep, give, block, beside, wide_hi, wide_lo, right2, half, square, flat, sems
):
    rows, cols, _ = block.shape
    active, pairs = turned_orbitals.shape[0], out.shape[0]
    steps = sems.shape[1]
    tall = rows // steps

    def fetch(kind, step):
        part = pl.ds(step * tall, tall)
        source, target = ((vectors, block), (columns, beside))[kind]
        return pltpu.make_async_copy(source.at[part], target.at[part], sems.at[kind, step])

    for kind in range(2):
        for step in range(steps):
            fetch(kind, step).start()

    index_mu = me[0] >> 3
    left = turned_orbitals[:, pl.ds(pl.multiple_of((index_mu >> 1) * LANES, LANES), LANES)]
    right = turned_orbitals[:, pl.ds(pl.multiple_of((me[0] & 7) * cols, cols), cols)]
    high = (active * 8, active)
    spread_rows = jnp.where(iota(high, 0) // 8 == iota(high, 1), 1.0, 0.0).astype(bf16)
    long = (LANES, rows * 8)
    spread_cols = jnp.where(iota(long, 0) == iota(long, 1) // 8 + (index_mu & 1) * rows, 1.0, 0.0).astype(bf16)
    full = (active * 8, rows * 8)
    same = iota(full, 0) % 8 == iota(full, 1) % 8
    for part, wide in zip(split(left), (wide_hi, wide_lo)):
        repeated = dot(dot(spread_rows, part).astype(bf16), spread_cols)
        wide[...] = jnp.where(same, repeated, 0.0).astype(bf16)
    eye = jnp.where(iota((48, active), 0) == iota((48, active), 1), 1.0, 0.0).astype(bf16)
    upper, lower = [dot(eye, part).astype(bf16) for part in split(right)]
    right2[:48, :cols] = upper
    right2[:48, cols:] = upper
    right2[48:, :cols] = lower
    right2[48:, cols:] = jnp.zeros_like(lower)

    for kind, (value, target) in enumerate(((block, out), (beside, flat))):
        width = value.shape[2]

        def advance(step, carry):
            fetch(kind, step).wait()
            for i in range(tall):
                row = step * tall + i
                both = dot(right2[...], jnp.concatenate(split(value[row]), axis=0))
                half[row, :, :width] = both[:active] + both[48 : 48 + active]
            return carry

        lax.fori_loop(0, steps, advance, 0)
        for q in range(0, active, 8):
            upper, lower = split(half[:, q : q + 8, :width].reshape(rows * 8, width))
            hi, lo = wide_hi[8 * q :, :], wide_lo[8 * q :, :]
            both = dot(jnp.concatenate([hi, lo], axis=0), upper)
            part = both[: 8 * (active - q)] + both[8 * (active - q) :] + dot(hi, lower)
            square[q:, q : q + 8, :width] = part.reshape(active - q, 8, width)
        for p in range(active):
            target[p * (p + 1) // 2 : (p + 1) * (p + 2) // 2, :] = square[p, : p + 1, :width]

    turned = flat[...].T[:, :pairs]
    first = (index_mu & 1) == 0
    for i in range(8):
        a, b = turned[32 * i : 32 * i + 16], turned[32 * i + 16 : 32 * i + 32]
        keep[16 * i : 16 * i + 16, :] = jnp.where(first, a, b)
        give[16 * i : 16 * i + 16, :] = jnp.where(first, b, a)


def turn(me, turned_orbitals, vectors, columns):
    rows, cols, depth = vectors.shape
    count = columns.shape[2]
    active = turned_orbitals.shape[0]
    pairs = active * (active + 1) // 2
    steps = 8
    return pl.pallas_call(
        turn_kernel,
        out_shape=(
            jax.ShapeDtypeStruct((pairs, depth), f32),
            jax.ShapeDtypeStruct((count // 2, pairs), f32),
            jax.ShapeDtypeStruct((count // 2, pairs), f32),
        ),
        in_specs=[smem, vmem, hbm, hbm],
        out_specs=(vmem,) * 3,
        scratch_shapes=[
            pltpu.VMEM(vectors.shape, f32),
            pltpu.VMEM(columns.shape, f32),
            pltpu.VMEM((active * 8, rows * 8), bf16),
            pltpu.VMEM((active * 8, rows * 8), bf16),
            pltpu.VMEM((96, 2 * cols), bf16),
            pltpu.VMEM((rows, active, depth), f32),
            pltpu.VMEM((active, active, depth), f32),
            pltpu.VMEM((pl.cdiv(pairs, LANES) * LANES, count), f32),
            pltpu.SemaphoreType.DMA((2, steps)),
        ],
        compiler_params=params(56),
        cost_estimate=pl.CostEstimate(
            flops=10**10, bytes_accessed=4 * (vectors.size + columns.size), transcendentals=0
        ),
        name="turn",
    )(me, turned_orbitals, vectors, columns)


def unpack(packed):
    rows = packed.shape[0] * packed.shape[1]
    depth = (packed.shape[2] - LANES) // PER_ROW
    flat = packed[...].reshape(rows, packed.shape[2])
    vectors = [flat[:, depth * i : depth * (i + 1)] for i in range(PER_ROW)]
    spots = [depth * PER_ROW + LANES // PER_ROW * i for i in range(PER_ROW)]
    scales = [jnp.broadcast_to(flat[:, spot : spot + 1], (rows, LANES)) for spot in spots]
    return jnp.concatenate([jnp.concatenate(vectors, axis=0), jnp.concatenate(scales, axis=0)], axis=1)


def choose_kernel(
    me, near_hot, far_hot, near, far, upper_v, lower_v, mine_c, got_c, part, rows_out, scale_out, rows_all, scaling, keep_hi, keep_lo, sems
):
    depth = rows_all.shape[1]
    width = depth + LANES
    count = near_hot.shape[0]
    core = (me[0] >> 3) & 1
    near_hi, near_lo = split(unpack(near))
    far_hi, far_lo = split(unpack(far))
    hi = dot(near_hot[...], near_hi) + dot(far_hot[...], far_hi)
    lo = dot(near_hot[...], near_lo) + dot(far_hot[...], far_lo)
    hi16, lo16 = hi.astype(bf16), lo.astype(bf16)
    rows_all[:count, :] = hi16[:, :depth]
    rows_all[count:, :] = lo16[:, :depth]
    scaling[...] = (hi[:, depth:] + lo[:, depth:]).T[:8]
    copies = [
        pltpu.make_async_copy(rows_all, rows_out, sems.at[0]),
        pltpu.make_async_copy(scaling, scale_out, sems.at[1]),
    ]
    for copy in copies:
        copy.start()
    keep_hi[...] = hi16.reshape(keep_hi.shape)
    keep_lo[...] = lo16.reshape(keep_lo.shape)
    home_hi = keep_hi[:, core].reshape(-1, width)
    home_lo = keep_lo[:, core].reshape(-1, width)
    moved = (
        dot_nt(home_hi[:, :depth], upper_v[...])
        + dot_nt(home_lo[:, :depth], upper_v[...])
        + dot_nt(home_hi[:, :depth], lower_v[...])
    )
    scale = home_hi[:, depth : depth + 1].astype(f32) + home_lo[:, depth : depth + 1].astype(f32)
    part[...] = ((mine_c[...] + got_c[...] - moved) * scale).reshape(part.shape)
    for copy in copies:
        copy.wait()


def choose(me, near_hot, far_hot, near, far, upper_v, lower_v, mine_c, got_c):
    count, slots = near_hot.shape
    depth = upper_v.shape[1]
    width = depth + LANES
    pairs = upper_v.shape[0]
    return pl.pallas_call(
        choose_kernel,
        out_shape=(
            jax.ShapeDtypeStruct((64, count // 128, pairs), f32),
            pltpu.HBM((2 * count, depth), bf16),
            pltpu.HBM((8, count), f32),
        ),
        in_specs=[smem] + [vmem] * 8,
        out_specs=(vmem, pl.BlockSpec(memory_space=pltpu.HBM), pl.BlockSpec(memory_space=pltpu.HBM)),
        scratch_shapes=[
            pltpu.VMEM((2 * count, depth), bf16),
            pltpu.VMEM((8, count), f32),
            pltpu.VMEM((8, 2, 16, width), bf16),
            pltpu.VMEM((8, 2, 16, width), bf16),
            pltpu.SemaphoreType.DMA((2,)),
        ],
        compiler_params=params(24),
        cost_estimate=pl.CostEstimate(flops=2 * 10**9, bytes_accessed=6 * 10**6, transcendentals=0),
        name="choose",
    )(me, near_hot, far_hot, near, far, upper_v, lower_v, mine_c, got_c)


def update_kernel(vectors, columns, diagonal, rows_all, scaling, out, block, beside, sems):
    rows, cols, depth = block.shape
    count = beside.shape[2]
    steps = sems.shape[1]
    tall = rows // steps

    def fetch(step):
        part = pl.ds(step * tall, tall)
        return (
            pltpu.make_async_copy(vectors.at[part], block.at[part], sems.at[0, step]),
            pltpu.make_async_copy(columns.at[part], beside.at[part], sems.at[1, step]),
        )

    for step in range(steps):
        for copy in fetch(step):
            copy.start()

    def advance(step, carry):
        for copy in fetch(step):
            copy.wait()
        part = pl.ds(pl.multiple_of(step * tall, tall), tall)
        upper, lower = split(block[part].reshape(tall * cols, depth))
        both = dot_nt(upper, rows_all[...])
        update = both[:, :count] + both[:, count:] + dot_nt(lower, rows_all[:count, :])
        fresh = (beside[part].reshape(tall * cols, count) - update) * scaling[:1, :]
        square = fresh * fresh
        folded = (square[:, :LANES] + square[:, LANES:]).reshape(tall, cols, LANES)
        out[part, :] = diagonal[part, :] - jnp.sum(jnp.swapaxes(folded, 1, 2), axis=1)
        return carry

    lax.fori_loop(0, steps, advance, 0)


def update(vectors, columns, diagonal, rows_all, scaling):
    rows, cols, depth = vectors.shape
    count = columns.shape[2]
    steps = 8
    return pl.pallas_call(
        update_kernel,
        out_shape=jax.ShapeDtypeStruct((rows, cols), f32),
        in_specs=[hbm, hbm, vmem, vmem, vmem],
        out_specs=vmem,
        scratch_shapes=[
            pltpu.VMEM(vectors.shape, f32),
            pltpu.VMEM(columns.shape, f32),
            pltpu.SemaphoreType.DMA((2, steps)),
        ],
        compiler_params=params(56),
        cost_estimate=pl.CostEstimate(
            flops=6 * rows * cols * depth * count, bytes_accessed=4 * (vectors.size + columns.size), transcendentals=0
        ),
        name="update",
    )(vectors, columns, diagonal, rows_all, scaling)


def local(vectors, columns, diagonal, orbitals, pivots):
    count = pivots.shape[0]
    core = lax.axis_index("c")
    me = lax.axis_index(("y", "zh", "c", "zl", "x")).reshape(1)
    near = exchange(pick(me, pivots, diagonal, vectors), PEERS)

    own_chip, own_core = (pivots >> 17) * 8 + ((pivots & 1023) >> 7), (pivots >> 16) & 1
    block = own_chip * 2 + own_core
    order = jnp.arange(count)
    rank = jnp.sum((block[None, :] == block[:, None]) & (order[None, :] < order[:, None]), axis=1)
    spot = rank % PER_ROW * (64 * SLOTS // PER_ROW) + own_chip * (SLOTS // PER_ROW) + rank // PER_ROW
    place = jnp.where(own_core == core, spot, -1)
    other = jnp.where(own_core == core, -1, spot)
    slot = jnp.arange(64 * SLOTS)
    near_hot = (place[:, None] == slot[None, :]).astype(bf16)
    far_hot = (other[:, None] == slot[None, :]).astype(bf16)

    mine_v, keep_c, give_c = turn(me, orbitals.T, vectors, columns)
    got_v, got_c = sibling(mine_v), sibling(give_c)
    chip_v = mine_v + got_v
    upper_v = lax.reduce_precision(chip_v, 8, 7)
    lower_v = (chip_v - upper_v).astype(bf16)
    upper_v = upper_v.astype(bf16)

    near, keep_c, near_hot, far_hot = lax.optimization_barrier((near, keep_c, near_hot, far_hot))
    far = sibling(near)
    part, rows_all, scaling = choose(me, near_hot, far_hot, near, far, upper_v, lower_v, keep_c, got_c)
    arrived = exchange(part, PEERS)
    updated = update(vectors, columns, diagonal, rows_all, scaling)
    return arrived.sum(axis=0), updated


def solution(mesh):
    fine = Mesh(mesh.devices.reshape(4, 2, 2, 2, 4), ("y", "zh", "c", "zl", "x"))
    mu, nu = ("y", "zh", "c"), ("zl", "x")
    placed = (P(mu, nu, None), P(mu, nu, None), P(mu, nu), P(), P())
    return jax.shard_map(
        local,
        mesh=fine,
        in_specs=placed,
        out_specs=(P(mu + nu, None), P(mu, nu)),
        check_vma=False,
    )
```
